32 devices in a mesh: group: 1, rows: 32 (over z, y, x, core).
Axes of the slice: x: 2, y: 2, z: 4, core: 2. Of those that a mesh axis runs over, the one named last changes fastest.
Arguments:
- embeddings: float32 [12288, 4096], P(('group', 'rows'))
- assignment: int32 [12288], P(('group', 'rows')), may hold values from 0 to 255, as said below
Outputs:
- maxima: float32 [12288], P(('group', 'rows'))
- centroids: float32 [256, 4096], P(('group', 'rows'))
The draws below stay inside these ranges and needn't reach their ends.
Inputs may be any that keep to these rules, and one draw needn't show every extreme that they name: `assignment`: on each index of rows (384 rows in order) no cluster has more than 2 rows, and some cluster has exactly 2 rows on every index; every cluster has at least one row.
All inputs are finite; a program needn't handle non-finite values.
Results may differ from the reference program's by a relative error of at most 0.0003.
Values may be sent and summed in bfloat16 or wider, within the bound.
No kernel may reach another device: no remote copies, remote signals or barrier semaphores. Data moves between devices by JAX's collectives and lax.ppermute only.
A program may use at most 64 MiB of HBM per device.

```python
import math
import jax
import jax.numpy as jnp
from jax import lax

D = 4096
CLUSTERS = 256
R_DEV = 384
SLOTS = 2
NROWS = 12288
N_ROWS = 32


def cluster_draw(key):
    dev_count = NROWS // R_DEV
    cand_total = CLUSTERS * SLOTS
    cand_ids = jnp.arange(cand_total, dtype=jnp.int32)
    cand_cluster = cand_ids // SLOTS
    copy_index = cand_ids % SLOTS
    shuffled = jax.random.permutation(jax.random.fold_in(key, 101), CLUSTERS)
    cluster_rank = jnp.argsort(shuffled, stable=True).astype(jnp.int32)
    popularity = (CLUSTERS - cluster_rank) * (4096 // CLUSTERS)
    common_score = popularity[cand_cluster] - copy_index * 256 + jnp.where(cluster_rank[cand_cluster] == 0, 16384, 0)

    def per_device(device_idx):
        noise_key = jax.random.fold_in(jax.random.fold_in(key, 103), device_idx)
        order_key = jax.random.fold_in(jax.random.fold_in(key, 107), device_idx)
        jitter = jax.random.randint(noise_key, (cand_total,), 0, 1024)
        sure_one = (cand_cluster % dev_count == device_idx) & (copy_index == 0)
        scores = common_score + jitter + jnp.where(sure_one, 32768, 0)
        distinct = scores * cand_total + (cand_total - 1 - cand_ids)
        unused, picked = lax.top_k(distinct, R_DEV)
        chosen = cand_cluster[picked]
        reorder = jax.random.permutation(order_key, R_DEV)
        return chosen[reorder]
    per_rows = jax.vmap(per_device)(jnp.arange(dev_count, dtype=jnp.int32))
    return per_rows.reshape(-1).astype(jnp.int32)


def draw_assignment(key, part):
    return cluster_draw(key)


def draw_embeddings(key, part):
    assignment = cluster_draw(key)
    row_total = NROWS
    family = jax.random.randint(jax.random.fold_in(key, 201), (row_total,), 0, 256)
    amplitude = jnp.exp(jax.random.uniform(jax.random.fold_in(key, 203), (row_total,), jnp.float32, math.log(0.3), math.log(3.0)))
    top_scale = math.log(10.0)
    row_scale = jnp.exp(jax.random.uniform(jax.random.fold_in(key, 205), (row_total,), jnp.float32, 0.0, top_scale))
    column_gain = jnp.exp(jax.random.uniform(jax.random.fold_in(key, 207), (D,), jnp.float32, math.log(0.3), math.log(3.0)))
    cluster_key = jax.random.fold_in(key, 211)
    family_key = jax.random.fold_in(key, 213)
    noise_key = jax.random.fold_in(key, 215)

    def one_row(packed):
        row_id, cluster, fam, amp, scale = packed
        cluster_part = jax.random.normal(jax.random.fold_in(cluster_key, cluster), (D,), jnp.float32)
        family_part = jax.random.normal(jax.random.fold_in(family_key, cluster * 256 + fam), (D,), jnp.float32)
        own_part = jax.random.normal(jax.random.fold_in(noise_key, row_id), (D,), jnp.float32)
        return scale * column_gain * (2.0 * cluster_part + amp * family_part + own_part)
    row_ids = jnp.arange(row_total, dtype=jnp.int32)
    return lax.map(one_row, (row_ids, assignment, family, amplitude, row_scale)).astype(jnp.float32)


def setup_inputs(seed: int = 0, part: int = 0) -> dict:
    streams_of = jax.random.split(jax.random.key(seed), 3)
    part_keys = jax.random.split(jax.random.fold_in(streams_of[2], part), 3)
    return {
        "embeddings": draw_embeddings(jax.random.fold_in(jax.random.fold_in(streams_of[2], part), 71), part),
        "assignment": draw_assignment(jax.random.fold_in(jax.random.fold_in(streams_of[2], part), 71), part),
    }


def reference(embeddings, assignment):
    row_total = embeddings.shape[0]
    block_rows = 128
    row_ones = jnp.ones((row_total,), jnp.float32)
    counts = jax.ops.segment_sum(row_ones, assignment, num_segments=CLUSTERS)
    cluster_sums = jax.ops.segment_sum(embeddings, assignment, num_segments=CLUSTERS)
    centroids = cluster_sums / counts[:, None]
    centred = embeddings - centroids[assignment]
    unit = (centred * lax.rsqrt(lax.optimization_barrier(jnp.mean(centred * centred, axis=1, keepdims=True)) + 1e-06)).astype(jnp.bfloat16)
    ordering = jnp.argsort(assignment, stable=True).astype(jnp.int32)
    int_ones = jnp.ones((row_total,), jnp.int32)
    members_n = jax.ops.segment_sum(int_ones, assignment, num_segments=CLUSTERS).astype(jnp.int32)
    offsets = (jnp.cumsum(members_n) - members_n).astype(jnp.int32)
    padded = jnp.concatenate([unit[ordering], jnp.zeros((block_rows, unit.shape[1]), unit.dtype)], axis=0)
    span = N_ROWS * SLOTS
    tile_ids = jnp.arange(block_rows, dtype=jnp.int32)

    def per_cluster(cluster):
        first_row = offsets[cluster]
        members = members_n[cluster]
        block_count = (members + block_rows - 1) // block_rows

        def query_step(query_idx, result):
            query_start = (query_idx * block_rows).astype(jnp.int32)
            query = lax.dynamic_slice_in_dim(padded, first_row + query_start, block_rows, 0)
            query_ids = query_start + tile_ids

            def key_step(key_idx, best):
                key_start = (key_idx * block_rows).astype(jnp.int32)
                keys = lax.dynamic_slice_in_dim(padded, first_row + key_start, block_rows, 0)
                key_ids = key_start + tile_ids
                scores = jnp.dot(query, keys.T, preferred_element_type=jnp.float32) / D
                usable = (key_ids[None, :] < members) & (key_ids[None, :] != query_ids[:, None])
                return jnp.maximum(best, lax.optimization_barrier(jnp.max(jnp.where(usable, scores, -1.0), axis=1)))
            best = lax.fori_loop(0, block_count, key_step, jnp.full((block_rows,), -1.0, jnp.float32))
            return lax.dynamic_update_slice_in_dim(result, best, query_start, 0)
        result = lax.fori_loop(0, block_count, query_step, jnp.full((span + block_rows,), -1.0, jnp.float32))
        return result[:span]
    table = lax.map(per_cluster, jnp.arange(CLUSTERS, dtype=jnp.int32))
    sorted_cluster = assignment[ordering]
    local_index = (jnp.arange(row_total, dtype=jnp.int32) - offsets[sorted_cluster]).astype(jnp.int32)
    values = table[sorted_cluster, local_index]
    maxima = jnp.zeros((row_total,), jnp.float32).at[ordering].set(values)
    return (maxima, centroids)
```

```python
import functools

import jax
import jax.numpy as jnp
from jax import lax
from jax.experimental import pallas as pl
from jax.experimental.pallas import tpu as pltpu
from jax.sharding import PartitionSpec as P

CLUSTERS = 256
TILE = 512
LANES = 128
PARTS = (1024, 1024, 2048)
F32 = jnp.float32
BF16 = jnp.bfloat16


def iota(shape, axis):
    return lax.broadcasted_iota(jnp.int32, shape, axis)


def mm(a, b):
    return lax.dot_general(a, b, (((1,), (0,)), ((), ())), preferred_element_type=F32)


def to_row(col):
    n = col.shape[0]
    return jnp.sum(jnp.where(iota((n, n), 0) == iota((n, n), 1), col, 0), axis=0, keepdims=True)


def to_col(row):
    n = row.shape[1]
    return jnp.sum(jnp.where(iota((n, n), 0) == iota((n, n), 1), row, 0), axis=1, keepdims=True)


def pack_kernel(assign_ref, x_ref, out_ref, mix_ref, count_ref):
    rows = x_ref.shape[0]
    tile = x_ref.shape[1]

    @pl.when(pl.program_id(0) == 0)
    def _():
        a_row = assign_ref[...]
        a_col = to_col(a_row)
        twin = (a_col == a_row) & (iota((rows, rows), 0) < iota((rows, rows), 1))
        second = jnp.sum(twin.astype(F32), axis=0, keepdims=True)
        member = iota((CLUSTERS, rows), 0) == a_row
        count = jnp.sum(member.astype(F32), axis=1, keepdims=True)
        count_ref[...] = count
        share = jnp.where(count > 1.5, 0.5, 1.0)
        mix_ref[:CLUSTERS] = jnp.where(member, share, 0.0).astype(BF16)
        sign = jnp.where(second > 0.5, -0.5, 0.5)
        mix_ref[CLUSTERS:] = jnp.where(member & (count > 1.5), sign, 0.0).astype(BF16)

    x = x_ref[...]
    high = x.astype(BF16)
    low = (x - high.astype(F32)).astype(BF16)
    mixed = mm(mix_ref[...], high) + mm(mix_ref[...], low)
    mean = mixed[:CLUSTERS]
    half = mixed[CLUSTERS:]
    count = count_ref[...]
    mean_high = mean.astype(BF16)
    mean_low = (mean - mean_high.astype(F32)).astype(BF16)
    out_ref[:, :tile] = jnp.where(count > 0.5, mean_high.astype(F32), jnp.inf).astype(BF16)
    out_ref[:, tile : 2 * tile] = mean_low
    out_ref[:, 2 * tile :] = jnp.where(count > 1.5, half, jnp.inf).astype(BF16)


def pack(assign_row, x, start, width):
    rows = x.shape[0]
    first = start // TILE
    return pl.pallas_call(
        pack_kernel,
        grid=(width // TILE,),
        in_specs=[
            pl.BlockSpec((1, rows), lambda t: (0, 0)),
            pl.BlockSpec((rows, TILE), lambda t: (0, first + t)),
        ],
        out_specs=pl.BlockSpec((CLUSTERS, 3 * TILE), lambda t: (0, t)),
        out_shape=jax.ShapeDtypeStruct((CLUSTERS, 3 * width), BF16),
        scratch_shapes=[pltpu.VMEM((2 * CLUSTERS, rows), BF16), pltpu.VMEM((CLUSTERS, 1), F32)],
    )(assign_row, x)


def compare_kernel(cl_dev, width_all, last, *refs):
    if last:
        got_ref, gram_in_ref, centroid_ref, best_ref, gram_ref, mix_ref, total_ref, live_ref = refs
    else:
        got_ref, gram_in_ref, centroid_ref, gram_ref, mix_ref, total_ref, live_ref = refs
        best_ref = None
    slots = got_ref.shape[0]
    tile = got_ref.shape[1] // 3

    @pl.when(pl.program_id(0) == 0)
    def _():
        gram_ref[...] = gram_in_ref[...]
        live0 = (got_ref[:, :1].astype(F32) < jnp.inf).astype(F32)
        live1 = (got_ref[:, 2 * tile : 2 * tile + 1].astype(F32) < jnp.inf).astype(F32)
        live_ref[:slots] = live0
        live_ref[slots:] = live1
        same = (iota((slots, slots), 0) % cl_dev) == (iota((slots, slots), 1) % cl_dev)
        mix = jnp.where(same, to_row(live0 + live1), 0.0)
        mix_ref[...] = mix.astype(BF16)
        total_ref[...] = jnp.sum(mix, axis=1, keepdims=True)

    live0 = live_ref[:slots] > 0.5
    live1 = live_ref[slots:] > 0.5
    high = jnp.where(live0, got_ref[:, :tile].astype(F32), 0.0)
    low = got_ref[:, tile : 2 * tile]
    half = jnp.where(live1, got_ref[:, 2 * tile :].astype(F32), 0.0)
    mix = mix_ref[...]
    centroid = (mm(mix, high.astype(BF16)) + mm(mix, low)) / total_ref[...]
    centroid_ref[...] = centroid[:cl_dev]
    away = (high - centroid) + low.astype(F32)
    both = jnp.concatenate([away + half, away - half], axis=0).astype(BF16)
    gram_ref[...] += lax.dot_general(both, both, (((1,), (1,)), ((), ())), preferred_element_type=F32)

    if last:

        @pl.when(pl.program_id(0) == pl.num_programs(0) - 1)
        def _():
            n = 2 * slots
            gram = gram_ref[...]
            row = iota((n, n), 0)
            col = iota((n, n), 1)
            diag = jnp.where(row == col, gram, 0.0)
            inv_row = lax.rsqrt(jnp.sum(diag, axis=0, keepdims=True) / width_all + 1e-6)
            inv_col = lax.rsqrt(jnp.sum(diag, axis=1, keepdims=True) / width_all + 1e-6)
            score = gram * inv_col * inv_row / width_all
            usable = ((row % cl_dev) == (col % cl_dev)) & (row != col) & (live_ref[...] > 0.5)
            best = jnp.max(jnp.where(usable, score, -1.0), axis=0, keepdims=True)
            sources = slots // cl_dev
            source = (iota((sources, n), 1) % slots) // cl_dev
            spread = jnp.where(source == iota((sources, n), 0), best, 0.0)
            slot = iota((n, LANES), 0)
            lane = (slot // slots) * cl_dev + slot % cl_dev
            pick = (lane == iota((n, LANES), 1)).astype(F32)
            best_ref[...] = lax.dot_general(
                spread,
                pick,
                (((1,), (0,)), ((), ())),
                precision=lax.Precision.HIGHEST,
                preferred_element_type=F32,
            )


def compare(got, gram, cl_dev, width_all, last):
    slots = got.shape[0]
    width = got.shape[1] // 3
    fixed = lambda t: (0, 0)
    out_shape = [jax.ShapeDtypeStruct((cl_dev, width), F32)]
    out_specs = [pl.BlockSpec((cl_dev, TILE), lambda t: (0, t))]
    scratch = [
        pltpu.VMEM((slots, slots), BF16),
        pltpu.VMEM((slots, 1), F32),
        pltpu.VMEM((2 * slots, 1), F32),
    ]
    if last:
        out_shape.append(jax.ShapeDtypeStruct((slots // cl_dev, LANES), F32))
        out_specs.append(pl.BlockSpec((slots // cl_dev, LANES), fixed))
        scratch.insert(0, pltpu.VMEM((2 * slots, 2 * slots), F32))
    else:
        out_shape.append(jax.ShapeDtypeStruct((2 * slots, 2 * slots), F32))
        out_specs.append(pl.BlockSpec((2 * slots, 2 * slots), fixed))
    return pl.pallas_call(
        functools.partial(compare_kernel, cl_dev, width_all, last),
        grid=(width // TILE,),
        in_specs=[
            pl.BlockSpec((slots, 3 * TILE), lambda t: (0, t)),
            pl.BlockSpec((2 * slots, 2 * slots), fixed),
        ],
        out_specs=out_specs,
        out_shape=out_shape,
        scratch_shapes=scratch,
    )(got, gram)


def on_device(embeddings, assignment):
    dev_count = lax.axis_size("rows")
    cl_dev = CLUSTERS // dev_count
    rows, width = embeddings.shape
    assign_row = assignment.reshape(1, rows)
    exchange = functools.partial(lax.all_to_all, axis_name="rows", split_axis=0, concat_axis=0, tiled=True)
    got = []
    start = 0
    for part in PARTS:
        got.append(exchange(pack(assign_row, embeddings, start, part)))
        start += part
    gram = jnp.zeros((2 * CLUSTERS, 2 * CLUSTERS), F32)
    centroids = []
    for i, piece in enumerate(got):
        c, gram = compare(piece, gram, cl_dev, width, i == len(got) - 1)
        centroids.append(c)
    found = exchange(gram)
    row_ids = jnp.arange(rows, dtype=jnp.int32)
    twin = (assignment[:, None] == assignment[None, :]) & (row_ids[None, :] < row_ids[:, None])
    second = jnp.sum(twin.astype(jnp.int32), axis=1)
    owner = (assignment // cl_dev)[:, None] == jnp.arange(dev_count, dtype=jnp.int32)[None, :]
    lane = (second * cl_dev + assignment % cl_dev)[:, None] == jnp.arange(LANES, dtype=jnp.int32)[None, :]
    lines = lax.dot_general(
        owner.astype(F32), found, (((1,), (0,)), ((), ())), precision=lax.Precision.HIGHEST
    )
    maxima = jnp.sum(jnp.where(lane, lines, 0.0), axis=1)
    return (maxima, jnp.concatenate(centroids, axis=1))


def solution(mesh):
    placed = (P(("group", "rows"), None), P(("group", "rows")))
    return jax.shard_map(
        on_device,
        mesh=mesh,
        in_specs=placed,
        out_specs=(P(("group", "rows")), P(("group", "rows"), None)),
        check_vma=False,
    )
```

```python
import functools

import jax
import jax.numpy as jnp
from jax import lax
from jax.experimental import pallas as pl
from jax.experimental.pallas import tpu as pltpu
from jax.sharding import PartitionSpec as P

CLUSTERS = 256
TILE = 512
LANES = 128
PARTS = (1024, 3072)
F32 = jnp.float32
BF16 = jnp.bfloat16


def iota(shape, axis):
    return lax.broadcasted_iota(jnp.int32, shape, axis)


def mm(a, b):
    return lax.dot_general(a, b, (((1,), (0,)), ((), ())), preferred_element_type=F32)


def to_row(col):
    n = col.shape[0]
    return jnp.sum(jnp.where(iota((n, n), 0) == iota((n, n), 1), col, 0), axis=0, keepdims=True)


def to_col(row):
    n = row.shape[1]
    return jnp.sum(jnp.where(iota((n, n), 0) == iota((n, n), 1), row, 0), axis=1, keepdims=True)


def gather_kernel(assign_ref, x_ref, sum_ref, half_ref, mix_ref):
    rows = x_ref.shape[0]

    @pl.when(pl.program_id(0) == 0)
    def _():
        a_row = assign_ref[...]
        a_col = to_col(a_row)
        twin = (a_col == a_row) & (iota((rows, rows), 0) < iota((rows, rows), 1))
        second = jnp.sum(twin.astype(F32), axis=0, keepdims=True)
        member = iota((CLUSTERS, rows), 0) == a_row
        count = jnp.sum(member.astype(F32), axis=1, keepdims=True)
        mix_ref[:CLUSTERS] = jnp.where(member, 1.0, 0.0).astype(BF16)
        sign = jnp.where(second > 0.5, -0.5, 0.5)
        mix_ref[CLUSTERS:] = jnp.where(member & (count > 1.5), sign, 0.0).astype(BF16)

    x = x_ref[...]
    high = x.astype(BF16)
    low = (x - high.astype(F32)).astype(BF16)
    mixed = mm(mix_ref[...], high) + mm(mix_ref[...], low)
    sum_ref[...] = mixed[:CLUSTERS]
    half_ref[...] = mixed[CLUSTERS:]


def gather(assign_row, x, start, width):
    rows = x.shape[0]
    first = start // TILE
    out = jax.ShapeDtypeStruct((CLUSTERS, width), F32)
    spec = pl.BlockSpec((CLUSTERS, TILE), lambda t: (0, t))
    return pl.pallas_call(
        gather_kernel,
        grid=(width // TILE,),
        in_specs=[
            pl.BlockSpec((1, rows), lambda t: (0, 0)),
            pl.BlockSpec((rows, TILE), lambda t: (0, first + t)),
        ],
        out_specs=[spec, spec],
        out_shape=[out, out],
        scratch_shapes=[pltpu.VMEM((2 * CLUSTERS, rows), BF16)],
    )(assign_row, x)


def code_kernel(core_ref, mine_ref, mate_ref, sum_ref, mate_sum_ref, half_ref, out_ref, count_ref):
    rows = mine_ref.shape[1]
    tile = sum_ref.shape[1]

    @pl.when(pl.program_id(0) == 0)
    def _():
        ids = iota((CLUSTERS, rows), 0)
        count_ref[:CLUSTERS] = jnp.sum((ids == mine_ref[...]).astype(F32), axis=1, keepdims=True)
        count_ref[CLUSTERS:] = jnp.sum((ids == mate_ref[...]).astype(F32), axis=1, keepdims=True)

    count = count_ref[:CLUSTERS]
    total = jnp.maximum(count + count_ref[CLUSTERS:], 1.0)
    sums = sum_ref[...]
    half = half_ref[...]
    mean = (sums + mate_sum_ref[...]) / total
    away = sums / jnp.maximum(count, 1.0) - mean
    high = mean.astype(BF16)
    low = (mean - high.astype(F32)).astype(BF16)

    @pl.when(core_ref[0] == 0)
    def _():
        out_ref[:, :tile] = jnp.where(count > 0.5, away + half, jnp.inf).astype(BF16)
        out_ref[:, tile : 2 * tile] = jnp.where(count > 1.5, away - half, jnp.inf).astype(BF16)
        out_ref[:, 2 * tile :] = low[:, : tile // 2]

    @pl.when(core_ref[0] == 1)
    def _():
        flag = jnp.where(count > 0.5, jnp.inf, -jnp.inf)
        out_ref[:, :tile] = jnp.where(count > 1.5, away - half, flag).astype(BF16)
        out_ref[:, tile : 2 * tile] = high
        out_ref[:, 2 * tile :] = low[:, tile // 2 :]


def code(core, mine, mate, sums, mate_sums, half):
    rows = mine.shape[1]
    width = sums.shape[1]
    wide = TILE * 5 // 2
    spec = pl.BlockSpec((CLUSTERS, TILE), lambda t: (0, t))
    line = pl.BlockSpec((1, rows), lambda t: (0, 0))
    return pl.pallas_call(
        code_kernel,
        grid=(width // TILE,),
        in_specs=[pl.BlockSpec(memory_space=pltpu.SMEM), line, line, spec, spec, spec],
        out_specs=pl.BlockSpec((CLUSTERS, wide), lambda t: (0, t)),
        out_shape=jax.ShapeDtypeStruct((CLUSTERS, width // TILE * wide), BF16),
        scratch_shapes=[pltpu.VMEM((2 * CLUSTERS, 1), F32)],
    )(core, mine, mate, sums, mate_sums, half)


def compare_kernel(cl_dev, width_all, first, last, *refs):
    refs = list(refs)
    even_ref, odd_ref = refs[:2]
    refs = refs[2:]
    gram_in_ref = None if first else refs.pop(0)
    centroid_ref = refs.pop(0)
    best_ref = refs.pop(0) if last else None
    gram_ref, mix_ref, total_ref, live_ref = refs
    slots = mix_ref.shape[0]
    tile = centroid_ref.shape[1]

    def part(ref, lo, hi):
        return ref[..., lo:hi].astype(F32).reshape(slots, hi - lo)

    @pl.when(pl.program_id(0) == 0)
    def _():
        gram_ref[...] = jnp.zeros_like(gram_ref) if first else gram_in_ref[...]
        mark = part(odd_ref, 0, LANES)[:, :1]
        live = [
            part(even_ref, 0, LANES)[:, :1] < jnp.inf,
            part(even_ref, tile, tile + LANES)[:, :1] < jnp.inf,
            mark > -jnp.inf,
            jnp.abs(mark) < jnp.inf,
        ]
        live = [x.astype(F32) for x in live]
        for k in range(4):
            live_ref[k * slots : (k + 1) * slots] = live[k]
        same = (iota((slots, slots), 0) % cl_dev) == (iota((slots, slots), 1) % cl_dev)
        mix = jnp.where(same, to_row(live[0] + live[1] + live[2] + live[3]), 0.0)
        mix_ref[...] = mix.astype(BF16)
        total_ref[...] = jnp.sum(mix, axis=1, keepdims=True)

    live = [live_ref[k * slots : (k + 1) * slots] > 0.5 for k in range(4)]
    d0 = jnp.where(live[0], part(even_ref, 0, tile), 0.0)
    d1 = jnp.where(live[1], part(even_ref, tile, 2 * tile), 0.0)
    d3 = jnp.where(live[3], part(odd_ref, 0, tile), 0.0)
    d2 = jnp.where(live[2], -(d0 + d1 + d3), 0.0)
    high = part(odd_ref, tile, 2 * tile)
    end = tile * 5 // 2
    low = jnp.concatenate([part(even_ref, 2 * tile, end), part(odd_ref, 2 * tile, end)], axis=1)
    mix = mix_ref[...]
    centroid = (mm(mix, high.astype(BF16)) + mm(mix, low.astype(BF16))) / total_ref[...]
    centroid_ref[...] = centroid[:cl_dev]
    away = (high - centroid) + low
    every = jnp.concatenate([away + d0, away + d1, away + d2, away + d3], axis=0).astype(BF16)
    gram_ref[...] += lax.dot_general(every, every, (((1,), (1,)), ((), ())), preferred_element_type=F32)

    if last:

        @pl.when(pl.program_id(0) == pl.num_programs(0) - 1)
        def _():
            n = 4 * slots
            gram = gram_ref[...]
            row = iota((n, n), 0)
            col = iota((n, n), 1)
            diag = jnp.where(row == col, gram, 0.0)
            inv_row = lax.rsqrt(jnp.sum(diag, axis=0, keepdims=True) / width_all + 1e-6)
            inv_col = lax.rsqrt(jnp.sum(diag, axis=1, keepdims=True) / width_all + 1e-6)
            score = gram * inv_col * inv_row / width_all
            usable = ((row % cl_dev) == (col % cl_dev)) & (row != col) & (live_ref[...] > 0.5)
            best = jnp.max(jnp.where(usable, score, -1.0), axis=0, keepdims=True)
            sources = 2 * slots // cl_dev
            place = iota((sources, n), 1)
            source = (place % slots) // cl_dev * 2 + place // (2 * slots)
            spread = jnp.where(source == iota((sources, n), 0), best, 0.0)
            place = iota((n, LANES), 0)
            lane = (place // slots) % 2 * cl_dev + place % cl_dev
            pick = (lane == iota((n, LANES), 1)).astype(F32)
            best_ref[...] = lax.dot_general(
                spread,
                pick,
                (((1,), (0,)), ((), ())),
                precision=lax.Precision.HIGHEST,
                preferred_element_type=F32,
            )


def compare(got, gram, cl_dev, width_all, last):
    first = gram is None
    slots = CLUSTERS // 2
    wide = TILE * 5 // 2
    width = got.shape[1] // wide * TILE
    chips = slots // cl_dev
    got = got.reshape(chips, 2, cl_dev, got.shape[1])
    fixed = lambda t: (0, 0)
    if cl_dev % 8 == 0:
        pair = [got, got]
        pair_specs = [
            pl.BlockSpec((chips, None, cl_dev, wide), lambda t: (0, 0, 0, t)),
            pl.BlockSpec((chips, None, cl_dev, wide), lambda t: (0, 1, 0, t)),
        ]
    else:
        pair = [got[:, k].reshape(slots, -1) for k in range(2)]
        pair_specs = [pl.BlockSpec((slots, wide), lambda t: (0, t))] * 2
    square = (4 * slots, 4 * slots)
    if not first:
        pair.append(gram)
        pair_specs.append(pl.BlockSpec(square, fixed))
    out_shape = [jax.ShapeDtypeStruct((cl_dev, width), F32)]
    out_specs = [pl.BlockSpec((cl_dev, TILE), lambda t: (0, t))]
    scratch = [
        pltpu.VMEM((slots, slots), BF16),
        pltpu.VMEM((slots, 1), F32),
        pltpu.VMEM((4 * slots, 1), F32),
    ]
    if last:
        out_shape.append(jax.ShapeDtypeStruct((2 * chips, LANES), F32))
        out_specs.append(pl.BlockSpec((2 * chips, LANES), fixed))
        scratch.insert(0, pltpu.VMEM(square, F32))
    else:
        out_shape.append(jax.ShapeDtypeStruct(square, F32))
        out_specs.append(pl.BlockSpec(square, fixed))
    return pl.pallas_call(
        functools.partial(compare_kernel, cl_dev, width_all, first, last),
        grid=(width // TILE,),
        in_specs=pair_specs,
        out_specs=out_specs,
        out_shape=out_shape,
        scratch_shapes=scratch,
    )(*pair)


def on_device(embeddings, assignment):
    dev_count = lax.axis_size("rows")
    cl_dev = CLUSTERS // dev_count
    rows, width = embeddings.shape
    core = (lax.axis_index("rows") % 2).astype(jnp.int32).reshape(1)
    mine = assignment.reshape(1, rows)
    exchange = functools.partial(lax.all_to_all, axis_name="rows", split_axis=0, concat_axis=0, tiled=True)
    swap = functools.partial(lax.ppermute, axis_name="rows", perm=[(i, i ^ 1) for i in range(dev_count)])
    mate = swap(mine)
    got = []
    start = 0
    for part in PARTS:
        sums, half = gather(mine, embeddings, start, part)
        coded = code(core, mine, mate, sums, swap(sums), half)
        coded, embeddings = lax.optimization_barrier((coded, embeddings))
        got.append(exchange(coded))
        start += part
    gram = None
    centroids = []
    for i, piece in enumerate(got):
        c, gram = compare(piece, gram, cl_dev, width, i == len(got) - 1)
        centroids.append(c)
    found = exchange(gram)
    row_ids = jnp.arange(rows, dtype=jnp.int32)
    twin = (assignment[:, None] == assignment[None, :]) & (row_ids[None, :] < row_ids[:, None])
    second = jnp.sum(twin.astype(jnp.int32), axis=1)
    owner = (assignment // cl_dev)[:, None] == jnp.arange(dev_count, dtype=jnp.int32)[None, :]
    lane = (second * cl_dev + assignment % cl_dev)[:, None] == jnp.arange(LANES, dtype=jnp.int32)[None, :]
    lines = lax.dot_general(
        owner.astype(F32), found, (((1,), (0,)), ((), ())), precision=lax.Precision.HIGHEST
    )
    maxima = jnp.sum(jnp.where(lane, lines, 0.0), axis=1)
    return (maxima, jnp.concatenate(centroids, axis=1))


def solution(mesh):
    placed = (P(("group", "rows"), None), P(("group", "rows")))
    return jax.shard_map(
        on_device,
        mesh=mesh,
        in_specs=placed,
        out_specs=(P(("group", "rows")), P(("group", "rows"), None)),
        check_vma=False,
    )
```

```python
import functools

import jax
import jax.numpy as jnp
import numpy as np
from jax import lax
from jax.experimental import pallas as pl
from jax.experimental.pallas import tpu as pltpu
from jax.sharding import PartitionSpec as P

CLUSTERS = 256
TILE = 512
LANES = 128
PARTS = (512, 3584)
F32 = jnp.float32
BF16 = jnp.bfloat16


def iota(shape, axis):
    return lax.broadcasted_iota(jnp.int32, shape, axis)


def mm(a, b):
    return lax.dot_general(a, b, (((1,), (0,)), ((), ())), preferred_element_type=F32)


def to_row(col):
    n = col.shape[0]
    return jnp.sum(jnp.where(iota((n, n), 0) == iota((n, n), 1), col, 0), axis=0, keepdims=True)


def to_col(row):
    n = row.shape[1]
    return jnp.sum(jnp.where(iota((n, n), 0) == iota((n, n), 1), row, 0), axis=1, keepdims=True)


def code_kernel(core_ref, mine_ref, mate_ref, x_ref, y_ref, out_ref, sum_ref, own_ref, num_ref):
    rows, tile = x_ref.shape

    @pl.when(pl.program_id(0) == 0)
    def _():
        mine = mine_ref[...]
        twin = (to_col(mine) == mine) & (iota((rows, rows), 0) < iota((rows, rows), 1))
        second = jnp.sum(twin.astype(F32), axis=0, keepdims=True) > 0.5
        member = iota((CLUSTERS, rows), 0) == mine
        other = iota((CLUSTERS, rows), 0) == mate_ref[...]
        sum_ref[:, :rows] = member.astype(F32).astype(BF16)
        sum_ref[:, rows:] = other.astype(F32).astype(BF16)
        own_ref[:CLUSTERS] = (member & ~second).astype(F32).astype(BF16)
        own_ref[CLUSTERS:] = (member & second).astype(F32).astype(BF16)
        count = jnp.sum(member.astype(F32), axis=1, keepdims=True)
        total = count + jnp.sum(other.astype(F32), axis=1, keepdims=True)
        num_ref[:CLUSTERS] = count
        num_ref[CLUSTERS:] = 1.0 / jnp.maximum(total, 1.0)

    x = x_ref[...]
    y = y_ref[...]
    x_high = x.astype(BF16)
    x_low = (x - x_high.astype(F32)).astype(BF16)
    y_high = y.astype(BF16)
    y_low = (y - y_high.astype(F32)).astype(BF16)
    sums = mm(sum_ref[...], jnp.concatenate([x_high, y_high], axis=0))
    sums += mm(sum_ref[...], jnp.concatenate([x_low, y_low], axis=0))
    mean = sums * num_ref[CLUSTERS:]
    high = mean.astype(BF16)
    low = (mean - high.astype(F32)).astype(BF16)
    count = num_ref[:CLUSTERS]

    @pl.when(core_ref[0] == 0)
    def _():
        own = mm(own_ref[...], x_high) + mm(own_ref[...], x_low)
        out_ref[:, :tile] = jnp.where(count > 0.5, own[:CLUSTERS] - mean, jnp.inf).astype(BF16)
        out_ref[:, tile : 2 * tile] = jnp.where(count > 1.5, own[CLUSTERS:] - mean, jnp.inf).astype(BF16)
        out_ref[:, 2 * tile :] = low[:, : tile // 2]

    @pl.when(core_ref[0] == 1)
    def _():
        own = mm(own_ref[CLUSTERS:], x_high) + mm(own_ref[CLUSTERS:], x_low)
        flag = jnp.where(count > 0.5, jnp.inf, -jnp.inf)
        out_ref[:, :tile] = jnp.where(count > 1.5, own - mean, flag).astype(BF16)
        out_ref[:, tile : 2 * tile] = high
        out_ref[:, 2 * tile :] = low[:, tile // 2 :]


def code(core, mine, mate, x, y, start):
    rows, width = y.shape
    first = start // TILE
    steps = width // TILE
    wide = TILE * 5 // 2
    line = pl.BlockSpec((1, rows), lambda t: (0, 0))
    if steps == 1:
        y = pltpu.with_memory_space_constraint(y, pltpu.VMEM)
        y_spec = pl.BlockSpec(memory_space=pltpu.VMEM)
    else:
        y_spec = pl.BlockSpec((rows, TILE), lambda t: (0, t))
    return pl.pallas_call(
        code_kernel,
        grid=(steps,),
        in_specs=[
            pl.BlockSpec(memory_space=pltpu.SMEM),
            line,
            line,
            pl.BlockSpec((rows, TILE), lambda t: (0, first + t)),
            y_spec,
        ],
        out_specs=pl.BlockSpec((CLUSTERS, wide), lambda t: (0, t)),
        out_shape=jax.ShapeDtypeStruct((CLUSTERS, steps * wide), BF16),
        scratch_shapes=[
            pltpu.VMEM((CLUSTERS, 2 * rows), BF16),
            pltpu.VMEM((2 * CLUSTERS, rows), BF16),
            pltpu.VMEM((2 * CLUSTERS, 1), F32),
        ],
    )(core, mine, mate, x, y)


def compare_kernel(cl_dev, width_all, first, last, *refs):
    refs = list(refs)
    got_ref = refs.pop(0)
    gram_in_ref = None if first else refs.pop(0)
    centroid_ref = refs.pop(0)
    best_ref = refs.pop(0) if last else None
    gram_ref, mix_ref, total_ref, live_ref = refs
    slots = mix_ref.shape[0]
    tile = centroid_ref.shape[1]

    def part(core, lo, hi):
        return got_ref[:, core, :, lo:hi].astype(F32).reshape(slots, hi - lo)

    @pl.when(pl.program_id(0) == 0)
    def _():
        gram_ref[...] = jnp.zeros_like(gram_ref) if first else gram_in_ref[...]
        mark = part(1, 0, LANES)[:, :1]
        live = [
            part(0, 0, LANES)[:, :1] < jnp.inf,
            part(0, tile, tile + LANES)[:, :1] < jnp.inf,
            mark > -jnp.inf,
            jnp.abs(mark) < jnp.inf,
        ]
        live = [x.astype(F32) for x in live]
        for k in range(4):
            live_ref[k * slots : (k + 1) * slots] = live[k]
        same = (iota((slots, slots), 0) % cl_dev) == (iota((slots, slots), 1) % cl_dev)
        mix = jnp.where(same, to_row(live[0] + live[1] + live[2] + live[3]), 0.0)
        mix_ref[...] = mix.astype(BF16)
        total_ref[...] = 1.0 / jnp.sum(mix, axis=1, keepdims=True)

    live = [live_ref[k * slots : (k + 1) * slots] > 0.5 for k in range(4)]
    d0 = jnp.where(live[0], part(0, 0, tile), 0.0)
    d1 = jnp.where(live[1], part(0, tile, 2 * tile), 0.0)
    d3 = jnp.where(live[3], part(1, 0, tile), 0.0)
    d2 = jnp.where(live[2], -(d0 + d1 + d3), 0.0)
    high = part(1, tile, 2 * tile)
    end = tile * 5 // 2
    low = jnp.concatenate([part(0, 2 * tile, end), part(1, 2 * tile, end)], axis=1)
    mix = mix_ref[...]
    centroid = (mm(mix, high.astype(BF16)) + mm(mix, low.astype(BF16))) * total_ref[...]
    centroid_ref[...] = centroid[:cl_dev]
    away = (high - centroid) + low
    every = jnp.concatenate([away + d0, away + d1, away + d2, away + d3], axis=0).astype(BF16)
    gram_ref[...] += lax.dot_general(every, every, (((1,), (1,)), ((), ())), preferred_element_type=F32)

    if last:

        @pl.when(pl.program_id(0) == pl.num_programs(0) - 1)
        def _():
            n = 4 * slots
            gram = gram_ref[...]
            row = iota((n, n), 0)
            col = iota((n, n), 1)
            diag = jnp.where(row == col, gram, 0.0)
            inv_row = lax.rsqrt(jnp.sum(diag, axis=0, keepdims=True) / width_all + 1e-6)
            inv_col = lax.rsqrt(jnp.sum(diag, axis=1, keepdims=True) / width_all + 1e-6)
            score = gram * inv_col * inv_row / width_all
            usable = ((row % cl_dev) == (col % cl_dev)) & (row != col) & (live_ref[...] > 0.5)
            best = jnp.max(jnp.where(usable, score, -1.0), axis=0, keepdims=True)
            sources = 2 * slots // cl_dev
            place = iota((sources, n), 1)
            source = (place % slots) // cl_dev * 2 + place // (2 * slots)
            spread = jnp.where(source == iota((sources, n), 0), best, 0.0)
            place = iota((n, LANES), 0)
            lane = (place // slots) % 2 * cl_dev + place % cl_dev
            pick = (lane == iota((n, LANES), 1)).astype(F32)
            best_ref[...] = lax.dot_general(
                spread,
                pick,
                (((1,), (0,)), ((), ())),
                precision=lax.Precision.HIGHEST,
                preferred_element_type=F32,
            )


def compare(got, gram, cl_dev, width_all, last):
    first = gram is None
    slots = CLUSTERS // 2
    wide = TILE * 5 // 2
    width = got.shape[1] // wide * TILE
    chips = slots // cl_dev
    got = got.reshape(chips, 2, cl_dev, got.shape[1])
    if cl_dev % 8:
        got = jnp.moveaxis(got, 1, 0).reshape(1, 2, slots, got.shape[3])
    fixed = lambda t: (0, 0)
    args = [got]
    if width == TILE:
        args = [pltpu.with_memory_space_constraint(got, pltpu.VMEM)]
        specs = [pl.BlockSpec(memory_space=pltpu.VMEM)]
    else:
        specs = [pl.BlockSpec((*got.shape[:3], wide), lambda t: (0, 0, 0, t))]
    square = (4 * slots, 4 * slots)
    if not first:
        args.append(gram)
        specs.append(pl.BlockSpec(square, fixed))
    out_shape = [jax.ShapeDtypeStruct((cl_dev, width), F32)]
    out_specs = [pl.BlockSpec((cl_dev, TILE), lambda t: (0, t))]
    scratch = [
        pltpu.VMEM((slots, slots), BF16),
        pltpu.VMEM((slots, 1), F32),
        pltpu.VMEM((4 * slots, 1), F32),
    ]
    if last:
        out_shape.append(jax.ShapeDtypeStruct((2 * chips, LANES), F32))
        out_specs.append(pl.BlockSpec((2 * chips, LANES), fixed))
        scratch.insert(0, pltpu.VMEM(square, F32))
    else:
        out_shape.append(jax.ShapeDtypeStruct(square, F32))
        out_specs.append(pl.BlockSpec(square, fixed))
    return pl.pallas_call(
        functools.partial(compare_kernel, cl_dev, width_all, first, last),
        grid=(width // TILE,),
        in_specs=specs,
        out_specs=out_specs,
        out_shape=out_shape,
        scratch_shapes=scratch,
    )(*args)


def on_device(embeddings, assignment):
    dev_count = lax.axis_size("rows")
    cl_dev = CLUSTERS // dev_count
    rows, width = embeddings.shape
    core = (lax.axis_index("rows") % 2).astype(jnp.int32).reshape(1)
    mine = assignment.reshape(1, rows)
    exchange = functools.partial(lax.all_to_all, axis_name="rows", split_axis=0, concat_axis=0, tiled=True)
    swap = functools.partial(lax.ppermute, axis_name="rows", perm=[(i, i ^ 1) for i in range(dev_count)])
    mate = swap(assignment).reshape(1, rows)
    others = []
    for part, end in zip(PARTS, np.cumsum(PARTS)):
        piece = embeddings[:, end - part : end]
        if others:
            piece, others[-1] = lax.optimization_barrier((piece, others[-1]))
        others.append(swap(piece))
    got = []
    start = 0
    for i, part in enumerate(PARTS):
        coded = code(core, mine, mate, embeddings, others[i], start)
        coded, embeddings = lax.optimization_barrier((coded, embeddings))
        got.append(exchange(coded))
        start += part
    gram = None
    centroids = []
    for i, piece in enumerate(got):
        c, gram = compare(piece, gram, cl_dev, width, i == len(got) - 1)
        centroids.append(c)
    found = exchange(gram)
    row_ids = jnp.arange(rows, dtype=jnp.int32)
    twin = (assignment[:, None] == assignment[None, :]) & (row_ids[None, :] < row_ids[:, None])
    second = jnp.sum(twin.astype(jnp.int32), axis=1)
    owner = (assignment // cl_dev)[:, None] == jnp.arange(dev_count, dtype=jnp.int32)[None, :]
    lane = (second * cl_dev + assignment % cl_dev)[:, None] == jnp.arange(LANES, dtype=jnp.int32)[None, :]
    lines = lax.dot_general(
        owner.astype(F32), found, (((1,), (0,)), ((), ())), precision=lax.Precision.HIGHEST
    )
    maxima = jnp.sum(jnp.where(lane, lines, 0.0), axis=1)
    return (maxima, jnp.concatenate(centroids, axis=1))


def solution(mesh):
    placed = (P(("group", "rows"), None), P(("group", "rows")))
    return jax.shard_map(
        on_device,
        mesh=mesh,
        in_specs=placed,
        out_specs=(P(("group", "rows")), P(("group", "rows"), None)),
        check_vma=False,
    )
```

```python
import functools

import jax
import jax.numpy as jnp
from jax import lax
from jax.experimental import pallas as pl
from jax.experimental.pallas import tpu as pltpu
from jax.sharding import PartitionSpec as P

CLUSTERS = 256
LANES = 128
PARTS = ((3584, 512, 512), (0, 3584, 1792))
F32 = jnp.float32
BF16 = jnp.bfloat16


def iota(shape, axis):
    return lax.broadcasted_iota(jnp.int32, shape, axis)


def mm(a, b):
    return lax.dot_general(a, b, (((1,), (0,)), ((), ())), preferred_element_type=F32)


def to_row(col):
    n = col.shape[0]
    return jnp.sum(jnp.where(iota((n, n), 0) == iota((n, n), 1), col, 0), axis=0, keepdims=True)


def to_col(row):
    n = row.shape[1]
    return jnp.sum(jnp.where(iota((n, n), 0) == iota((n, n), 1), row, 0), axis=1, keepdims=True)


def split(x):
    high = x.astype(BF16)
    return jnp.concatenate([high, (x - high.astype(F32)).astype(BF16)], axis=0)


def code_kernel(core_ref, mine_ref, mate_ref, x_ref, y_ref, out_ref, own_ref, other_ref, num_ref):
    rows, tile = x_ref.shape

    @pl.when(pl.program_id(0) == 0)
    def _():
        mine = mine_ref[...]
        twin = (to_col(mine) == mine) & (iota((rows, rows), 0) < iota((rows, rows), 1))
        second = jnp.sum(twin.astype(F32), axis=0, keepdims=True) > 0.5
        member = iota((CLUSTERS, rows), 0) == mine
        other = (iota((CLUSTERS, rows), 0) == mate_ref[...]).astype(F32)
        for k in range(2):
            cols = slice(k * rows, (k + 1) * rows)
            own_ref[:CLUSTERS, cols] = (member & ~second).astype(F32).astype(BF16)
            own_ref[CLUSTERS:, cols] = (member & second).astype(F32).astype(BF16)
            other_ref[:, cols] = other.astype(BF16)
        count = jnp.sum(member.astype(F32), axis=1, keepdims=True)
        total = count + jnp.sum(other, axis=1, keepdims=True)
        num_ref[:CLUSTERS] = count
        num_ref[CLUSTERS:] = 1.0 / jnp.maximum(total, 1.0)

    own = mm(own_ref[...], split(x_ref[...]))
    others = mm(other_ref[...], split(y_ref[...]))
    count = num_ref[:CLUSTERS]

    @pl.when(core_ref[0] == 0)
    def _():
        mean = ((own[:CLUSTERS] + own[CLUSTERS:]) + others) * num_ref[CLUSTERS:]
        low = (mean - mean.astype(BF16).astype(F32)).astype(BF16)
        out_ref[:, :tile] = jnp.where(count > 0.5, own[:CLUSTERS] - mean, jnp.inf).astype(BF16)
        out_ref[:, tile : 2 * tile] = jnp.where(count > 1.5, own[CLUSTERS:] - mean, jnp.inf).astype(BF16)
        out_ref[:, 2 * tile :] = low[:, : tile // 2]

    @pl.when(core_ref[0] == 1)
    def _():
        mean = ((own[:CLUSTERS] + own[CLUSTERS:]) + others) * num_ref[CLUSTERS:]
        high = mean.astype(BF16)
        low = (mean - high.astype(F32)).astype(BF16)
        flag = jnp.where(count > 0.5, jnp.inf, -jnp.inf)
        out_ref[:, :tile] = jnp.where(count > 1.5, own[CLUSTERS:] - mean, flag).astype(BF16)
        out_ref[:, tile : 2 * tile] = high
        out_ref[:, 2 * tile :] = low[:, tile // 2 :]


def code(core, mine, mate, x, y, start, width, tile):
    rows = x.shape[0]
    first = start // tile
    steps = width // tile
    wide = tile * 5 // 2
    line = pl.BlockSpec((1, rows), lambda t: (0, 0))
    block = pl.BlockSpec((rows, tile), lambda t: (0, first + t))
    if y.shape[1] == tile:
        y = pltpu.with_memory_space_constraint(y, pltpu.VMEM)
        y_spec = pl.BlockSpec(memory_space=pltpu.VMEM)
    else:
        y_spec = block
    return pl.pallas_call(
        code_kernel,
        grid=(steps,),
        in_specs=[pl.BlockSpec(memory_space=pltpu.SMEM), line, line, block, y_spec],
        out_specs=pl.BlockSpec((CLUSTERS, wide), lambda t: (0, t)),
        out_shape=jax.ShapeDtypeStruct((CLUSTERS, steps * wide), BF16),
        scratch_shapes=[
            pltpu.VMEM((2 * CLUSTERS, 2 * rows), BF16),
            pltpu.VMEM((CLUSTERS, 2 * rows), BF16),
            pltpu.VMEM((2 * CLUSTERS, 1), F32),
        ],
    )(core, mine, mate, x, y)


def compare_kernel(cl_dev, width_all, first, last, *refs):
    refs = list(refs)
    got_ref = refs.pop(0)
    gram_in_ref = None if first else refs.pop(0)
    centroid_ref = refs.pop(0)
    best_ref = refs.pop(0) if last else None
    gram_ref, mix_ref, total_ref, live_ref = refs
    slots = mix_ref.shape[0]
    tile = centroid_ref.shape[1]

    def part(core, lo, hi):
        return got_ref[:, core, :, lo:hi].astype(F32).reshape(slots, hi - lo)

    @pl.when(pl.program_id(0) == 0)
    def _():
        gram_ref[...] = jnp.zeros_like(gram_ref) if first else gram_in_ref[...]
        mark = part(1, 0, LANES)[:, :1]
        live = [
            part(0, 0, LANES)[:, :1] < jnp.inf,
            part(0, tile, tile + LANES)[:, :1] < jnp.inf,
            mark > -jnp.inf,
            jnp.abs(mark) < jnp.inf,
        ]
        live = [x.astype(F32) for x in live]
        for k in range(4):
            live_ref[k * slots : (k + 1) * slots] = live[k]
        same = (iota((slots, slots), 0) % cl_dev) == (iota((slots, slots), 1) % cl_dev)
        mix = jnp.where(same, to_row(live[0] + live[1] + live[2] + live[3]), 0.0)
        mix_ref[...] = mix.astype(BF16)
        total_ref[...] = 1.0 / jnp.sum(mix, axis=1, keepdims=True)

    live = [live_ref[k * slots : (k + 1) * slots] > 0.5 for k in range(4)]
    d0 = jnp.where(live[0], part(0, 0, tile), 0.0)
    d1 = jnp.where(live[1], part(0, tile, 2 * tile), 0.0)
    d3 = jnp.where(live[3], part(1, 0, tile), 0.0)
    d2 = jnp.where(live[2], -(d0 + d1 + d3), 0.0)
    high = part(1, tile, 2 * tile)
    end = tile * 5 // 2
    low = jnp.concatenate([part(0, 2 * tile, end), part(1, 2 * tile, end)], axis=1)
    mix = mix_ref[...]
    centroid = (mm(mix, high.astype(BF16)) + mm(mix, low.astype(BF16))) * total_ref[...]
    centroid_ref[...] = centroid[:cl_dev]
    away = (high - centroid) + low
    every = jnp.concatenate([away + d0, away + d1, away + d2, away + d3], axis=0).astype(BF16)
    gram_ref[...] += lax.dot_general(every, every, (((1,), (1,)), ((), ())), preferred_element_type=F32)

    if last:

        @pl.when(pl.program_id(0) == pl.num_programs(0) - 1)
        def _():
            n = 4 * slots
            gram = gram_ref[...]
            row = iota((n, n), 0)
            col = iota((n, n), 1)
            diag = jnp.where(row == col, gram, 0.0)
            inv_row = lax.rsqrt(jnp.sum(diag, axis=0, keepdims=True) / width_all + 1e-6)
            inv_col = lax.rsqrt(jnp.sum(diag, axis=1, keepdims=True) / width_all + 1e-6)
            score = gram * inv_col * inv_row / width_all
            usable = ((row % cl_dev) == (col % cl_dev)) & (row != col) & (live_ref[...] > 0.5)
            best = jnp.max(jnp.where(usable, score, -1.0), axis=0, keepdims=True)
            sources = 2 * slots // cl_dev
            place = iota((sources, n), 1)
            source = (place % slots) // cl_dev * 2 + place // (2 * slots)
            spread = jnp.where(source == iota((sources, n), 0), best, 0.0)
            place = iota((n, LANES), 0)
            lane = (place // slots) % 2 * cl_dev + place % cl_dev
            pick = (lane == iota((n, LANES), 1)).astype(F32)
            best_ref[...] = lax.dot_general(
                spread,
                pick,
                (((1,), (0,)), ((), ())),
                precision=lax.Precision.HIGHEST,
                preferred_element_type=F32,
            )


def compare(got, gram, cl_dev, width_all, last, tile):
    first = gram is None
    slots = CLUSTERS // 2
    wide = tile * 5 // 2
    width = got.shape[1] // wide * tile
    chips = slots // cl_dev
    got = got.reshape(chips, 2, cl_dev, got.shape[1])
    if cl_dev % 8:
        got = jnp.moveaxis(got, 1, 0).reshape(1, 2, slots, got.shape[3])
    fixed = lambda t: (0, 0)
    args = [got]
    if width == tile:
        args = [pltpu.with_memory_space_constraint(got, pltpu.VMEM)]
        specs = [pl.BlockSpec(memory_space=pltpu.VMEM)]
    else:
        specs = [pl.BlockSpec((*got.shape[:3], wide), lambda t: (0, 0, 0, t))]
    square = (4 * slots, 4 * slots)
    if not first:
        args.append(gram)
        specs.append(pl.BlockSpec(square, fixed))
    out_shape = [jax.ShapeDtypeStruct((cl_dev, width), F32)]
    out_specs = [pl.BlockSpec((cl_dev, tile), lambda t: (0, t))]
    scratch = [
        pltpu.VMEM((slots, slots), BF16),
        pltpu.VMEM((slots, 1), F32),
        pltpu.VMEM((4 * slots, 1), F32),
    ]
    if last:
        out_shape.append(jax.ShapeDtypeStruct((2 * chips, LANES), F32))
        out_specs.append(pl.BlockSpec((2 * chips, LANES), fixed))
        scratch.insert(0, pltpu.VMEM(square, F32))
    else:
        out_shape.append(jax.ShapeDtypeStruct(square, F32))
        out_specs.append(pl.BlockSpec(square, fixed))
    return pl.pallas_call(
        functools.partial(compare_kernel, cl_dev, width_all, first, last),
        grid=(width // tile,),
        in_specs=specs,
        out_specs=out_specs,
        out_shape=out_shape,
        scratch_shapes=scratch,
    )(*args)


def on_device(embeddings, assignment):
    dev_count = lax.axis_size("rows")
    cl_dev = CLUSTERS // dev_count
    rows, width = embeddings.shape
    core = (lax.axis_index("rows") % 2).astype(jnp.int32).reshape(1)
    mine = assignment.reshape(1, rows)
    exchange = functools.partial(lax.all_to_all, axis_name="rows", split_axis=0, concat_axis=0, tiled=True)
    swap = functools.partial(lax.ppermute, axis_name="rows", perm=[(i, i ^ 1) for i in range(dev_count)])
    mate = swap(assignment).reshape(1, rows)
    first, part, _ = PARTS[0]
    head = swap(embeddings[:, first : first + part])
    whole, head, mate = lax.optimization_barrier((embeddings, head, mate))
    tail = swap(whole)
    got = []
    for start, part, tile in PARTS:
        coded = code(core, mine, mate, embeddings, tail if got else head, start, part, tile)
        coded, embeddings = lax.optimization_barrier((coded, embeddings))
        got.append(exchange(coded))
    gram = None
    centroids = []
    for i, (_, _, tile) in enumerate(PARTS):
        c, gram = compare(got[i], gram, cl_dev, width, i == len(got) - 1, tile)
        centroids.append(c)
    found = exchange(gram)
    row_ids = jnp.arange(rows, dtype=jnp.int32)
    twin = (assignment[:, None] == assignment[None, :]) & (row_ids[None, :] < row_ids[:, None])
    second = jnp.sum(twin.astype(jnp.int32), axis=1)
    owner = (assignment // cl_dev)[:, None] == jnp.arange(dev_count, dtype=jnp.int32)[None, :]
    lane = (second * cl_dev + assignment % cl_dev)[:, None] == jnp.arange(LANES, dtype=jnp.int32)[None, :]
    lines = lax.dot_general(
        owner.astype(F32), found, (((1,), (0,)), ((), ())), precision=lax.Precision.HIGHEST
    )
    maxima = jnp.sum(jnp.where(lane, lines, 0.0), axis=1)
    return (maxima, jnp.concatenate(centroids[::-1], axis=1))


def solution(mesh):
    placed = (P(("group", "rows"), None), P(("group", "rows")))
    return jax.shard_map(
        on_device,
        mesh=mesh,
        in_specs=placed,
        out_specs=(P(("group", "rows")), P(("group", "rows"), None)),
        check_vma=False,
    )
```

```python
import functools

import jax
import jax.numpy as jnp
from jax import lax
from jax.experimental import pallas as pl
from jax.experimental.pallas import tpu as pltpu
from jax.sharding import PartitionSpec as P

CLUSTERS = 256
LANES = 128
PARTS = ((3840, 256, 128), (0, 3840, 640))
F32 = jnp.float32
BF16 = jnp.bfloat16


def iota(shape, axis):
    return lax.broadcasted_iota(jnp.int32, shape, axis)


def mm(a, b):
    return lax.dot_general(a, b, (((1,), (0,)), ((), ())), preferred_element_type=F32)


def to_row(col):
    n = col.shape[0]
    return jnp.sum(jnp.where(iota((n, n), 0) == iota((n, n), 1), col, 0), axis=0, keepdims=True)


def to_col(row):
    n = row.shape[1]
    return jnp.sum(jnp.where(iota((n, n), 0) == iota((n, n), 1), row, 0), axis=1, keepdims=True)


def split(x):
    high = x.astype(BF16)
    return jnp.concatenate([high, (x - high.astype(F32)).astype(BF16)], axis=0)


def code_kernel(core_ref, mine_ref, mate_ref, x_ref, y_ref, out_ref, pick0_ref, pick1_ref, num_ref):
    rows, tile = x_ref.shape
    core = core_ref[0]

    @pl.when(pl.program_id(0) == 0)
    def _():
        mine = mine_ref[...].reshape(1, rows)
        mate = mate_ref[...].reshape(1, rows)
        counts = []
        for k, pick_ref in enumerate((pick0_ref, pick1_ref)):
            ids = jnp.where(core == k, mine, mate)
            twin = (to_col(ids) == ids) & (iota((rows, rows), 0) < iota((rows, rows), 1))
            second = jnp.sum(twin.astype(F32), axis=0, keepdims=True) > 0.5
            member = iota((CLUSTERS, rows), 0) == ids
            upper = member & ~second if k == 0 else member
            for j in range(2):
                cols = slice(j * rows, (j + 1) * rows)
                pick_ref[:CLUSTERS, cols] = upper.astype(F32).astype(BF16)
                pick_ref[CLUSTERS:, cols] = (member & second).astype(F32).astype(BF16)
            counts.append(jnp.sum(member.astype(F32), axis=1, keepdims=True))
        num_ref[:CLUSTERS] = counts[0]
        num_ref[CLUSTERS : 2 * CLUSTERS] = counts[1]
        num_ref[2 * CLUSTERS :] = 1.0 / jnp.maximum(counts[0] + counts[1], 1.0)

    def body(x0_ref, x1_ref):
        rows0 = mm(pick0_ref[...], split(x0_ref[...]))
        rows1 = mm(pick1_ref[...], split(x1_ref[...]))
        count0 = num_ref[:CLUSTERS]
        count1 = num_ref[CLUSTERS : 2 * CLUSTERS]
        row0 = rows0[:CLUSTERS]
        row1 = rows0[CLUSTERS:]
        row3 = rows1[CLUSTERS:]
        mean = ((row0 + row1) + rows1[:CLUSTERS]) * num_ref[2 * CLUSTERS :]
        high = mean.astype(BF16)
        flag = jnp.where(count1 > 0.5, jnp.inf, -jnp.inf)
        out_ref[:, :tile] = jnp.where(count0 > 0.5, row0 - mean, jnp.inf).astype(BF16)
        out_ref[:, tile : 2 * tile] = jnp.where(count0 > 1.5, row1 - mean, jnp.inf).astype(BF16)
        out_ref[:, 2 * tile : 3 * tile] = jnp.where(count1 > 1.5, row3 - mean, flag).astype(BF16)
        out_ref[:, 3 * tile : 4 * tile] = high
        out_ref[:, 4 * tile :] = (mean - high.astype(F32)).astype(BF16)

    @pl.when(core == 0)
    def _():
        body(x_ref, y_ref)

    @pl.when(core == 1)
    def _():
        body(y_ref, x_ref)


def code(core, mine, mate, x, y, start, width, tile):
    rows = x.shape[0]
    first = start // tile
    steps = width // 2 // tile
    line = pl.BlockSpec((rows,), lambda t, core: (0,))
    block = pl.BlockSpec((rows, tile), lambda t, core: (0, first + core[0] * steps + t))
    if y.shape[1] == tile:
        y = pltpu.with_memory_space_constraint(y, pltpu.VMEM)
        y_spec = pl.BlockSpec(memory_space=pltpu.VMEM)
    else:
        y_spec = block
    return pl.pallas_call(
        code_kernel,
        grid_spec=pltpu.PrefetchScalarGridSpec(
            num_scalar_prefetch=1,
            grid=(steps,),
            in_specs=[line, pl.BlockSpec(memory_space=pltpu.VMEM), block, y_spec],
            out_specs=pl.BlockSpec((CLUSTERS, 5 * tile), lambda t, core: (0, t)),
            scratch_shapes=[
                pltpu.VMEM((2 * CLUSTERS, 2 * rows), BF16),
                pltpu.VMEM((2 * CLUSTERS, 2 * rows), BF16),
                pltpu.VMEM((3 * CLUSTERS, 1), F32),
            ],
        ),
        out_shape=jax.ShapeDtypeStruct((CLUSTERS, steps * 5 * tile), BF16),
    )(core, mine, pltpu.with_memory_space_constraint(mate, pltpu.VMEM), x, y)


def compare_kernel(cl_dev, width_all, first, last, *refs):
    refs = list(refs)
    got_ref = refs.pop(0)
    gram_in_ref = None if first else refs.pop(0)
    centroid_refs = [refs.pop(0), refs.pop(0)]
    best_ref = refs.pop(0) if last else None
    gram_ref, mix_ref, total_ref, live_ref = refs
    slots = mix_ref.shape[0]
    tile = centroid_refs[0].shape[1]

    def part(core, lo, hi):
        return got_ref[:, core, :, lo:hi].astype(F32).reshape(slots, hi - lo)

    @pl.when(pl.program_id(0) == 0)
    def _():
        gram_ref[...] = jnp.zeros_like(gram_ref) if first else gram_in_ref[...]
        mark = part(0, 2 * tile, 2 * tile + LANES)[:, :1]
        live = [
            part(0, 0, LANES)[:, :1] < jnp.inf,
            part(0, tile, tile + LANES)[:, :1] < jnp.inf,
            mark > -jnp.inf,
            jnp.abs(mark) < jnp.inf,
        ]
        live = [x.astype(F32) for x in live]
        for k in range(4):
            live_ref[k * slots : (k + 1) * slots] = live[k]
        same = (iota((slots, slots), 0) % cl_dev) == (iota((slots, slots), 1) % cl_dev)
        mix = jnp.where(same, to_row(live[0] + live[1] + live[2] + live[3]), 0.0)
        mix_ref[...] = mix.astype(BF16)
        total_ref[...] = 1.0 / jnp.sum(mix, axis=1, keepdims=True)

    live = [live_ref[k * slots : (k + 1) * slots] > 0.5 for k in range(4)]
    mix = mix_ref[...]
    scale = total_ref[...]
    gram = gram_ref[...]
    for core in range(2):
        d0 = jnp.where(live[0], part(core, 0, tile), 0.0)
        d1 = jnp.where(live[1], part(core, tile, 2 * tile), 0.0)
        d3 = jnp.where(live[3], part(core, 2 * tile, 3 * tile), 0.0)
        d2 = jnp.where(live[2], -(d0 + d1 + d3), 0.0)
        high = part(core, 3 * tile, 4 * tile)
        low = part(core, 4 * tile, 5 * tile)
        centroid = (mm(mix, high.astype(BF16)) + mm(mix, low.astype(BF16))) * scale
        centroid_refs[core][...] = centroid[:cl_dev]
        away = (high - centroid) + low
        every = jnp.concatenate([away + d0, away + d1, away + d2, away + d3], axis=0).astype(BF16)
        gram += lax.dot_general(every, every, (((1,), (1,)), ((), ())), preferred_element_type=F32)
    gram_ref[...] = gram

    if last:

        @pl.when(pl.program_id(0) == pl.num_programs(0) - 1)
        def _():
            n = 4 * slots
            gram = gram_ref[...]
            row = iota((n, n), 0)
            col = iota((n, n), 1)
            diag = jnp.where(row == col, gram, 0.0)
            inv_row = lax.rsqrt(jnp.sum(diag, axis=0, keepdims=True) / width_all + 1e-6)
            inv_col = lax.rsqrt(jnp.sum(diag, axis=1, keepdims=True) / width_all + 1e-6)
            score = gram * inv_col * inv_row / width_all
            usable = ((row % cl_dev) == (col % cl_dev)) & (row != col) & (live_ref[...] > 0.5)
            best = jnp.max(jnp.where(usable, score, -1.0), axis=0, keepdims=True)
            sources = 2 * slots // cl_dev
            place = iota((sources, n), 1)
            source = (place % slots) // cl_dev * 2 + place // (2 * slots)
            spread = jnp.where(source == iota((sources, n), 0), best, 0.0)
            place = iota((n, LANES), 0)
            lane = (place // slots) % 2 * cl_dev + place % cl_dev
            pick = (lane == iota((n, LANES), 1)).astype(F32)
            best_ref[...] = lax.dot_general(
                spread,
                pick,
                (((1,), (0,)), ((), ())),
                precision=lax.Precision.HIGHEST,
                preferred_element_type=F32,
            )


def compare(got, gram, cl_dev, width_all, last, tile):
    first = gram is None
    slots = CLUSTERS // 2
    half = got.shape[1] // 5
    chips = slots // cl_dev
    got = got.reshape(chips, 2, cl_dev, got.shape[1])
    if cl_dev % 8:
        got = jnp.moveaxis(got, 1, 0).reshape(1, 2, slots, got.shape[3])
    fixed = lambda t: (0, 0)
    args = [got]
    if half == tile:
        args = [pltpu.with_memory_space_constraint(got, pltpu.VMEM)]
        specs = [pl.BlockSpec(memory_space=pltpu.VMEM)]
    else:
        specs = [pl.BlockSpec((*got.shape[:3], 5 * tile), lambda t: (0, 0, 0, t))]
    square = (4 * slots, 4 * slots)
    if not first:
        args.append(gram)
        specs.append(pl.BlockSpec(square, fixed))
    out_shape = [jax.ShapeDtypeStruct((cl_dev, half), F32)] * 2
    out_specs = [pl.BlockSpec((cl_dev, tile), lambda t: (0, t))] * 2
    scratch = [
        pltpu.VMEM((slots, slots), BF16),
        pltpu.VMEM((slots, 1), F32),
        pltpu.VMEM((4 * slots, 1), F32),
    ]
    if last:
        out_shape.append(jax.ShapeDtypeStruct((2 * chips, LANES), F32))
        out_specs.append(pl.BlockSpec((2 * chips, LANES), fixed))
        scratch.insert(0, pltpu.VMEM(square, F32))
    else:
        out_shape.append(jax.ShapeDtypeStruct(square, F32))
        out_specs.append(pl.BlockSpec(square, fixed))
    return pl.pallas_call(
        functools.partial(compare_kernel, cl_dev, width_all, first, last),
        grid=(half // tile,),
        in_specs=specs,
        out_specs=out_specs,
        out_shape=out_shape,
        scratch_shapes=scratch,
    )(*args)


def on_device(embeddings, assignment):
    dev_count = lax.axis_size("rows")
    cl_dev = CLUSTERS // dev_count
    rows, width = embeddings.shape
    core = lax.axis_index("rows") % 2
    exchange = functools.partial(lax.all_to_all, axis_name="rows", split_axis=0, concat_axis=0, tiled=True)
    swap = functools.partial(lax.ppermute, axis_name="rows", perm=[(i, i ^ 1) for i in range(dev_count)])
    mate = swap(assignment)
    first, part, _ = PARTS[0]
    half = part // 2
    head = swap(lax.dynamic_slice_in_dim(embeddings, first + (1 - core) * half, half, 1))
    whole, head, mate = lax.optimization_barrier((embeddings, head, mate))
    tail = swap(whole)
    got = []
    for start, part, tile in PARTS:
        coded = code(core.astype(jnp.int32).reshape(1), assignment, mate, embeddings, tail if got else head, start, part, tile)
        coded, embeddings = lax.optimization_barrier((coded, embeddings))
        got.append(exchange(coded))
    gram = None
    centroids = []
    for i, (_, _, tile) in enumerate(PARTS):
        *c, gram = compare(got[i], gram, cl_dev, width, i == len(got) - 1, tile)
        centroids = c + centroids
    found = exchange(gram)
    row_ids = jnp.arange(rows, dtype=jnp.int32)
    twin = (assignment[:, None] == assignment[None, :]) & (row_ids[None, :] < row_ids[:, None])
    second = jnp.sum(twin.astype(jnp.int32), axis=1)
    owner = (assignment // cl_dev)[:, None] == jnp.arange(dev_count, dtype=jnp.int32)[None, :]
    lane = (second * cl_dev + assignment % cl_dev)[:, None] == jnp.arange(LANES, dtype=jnp.int32)[None, :]
    lines = lax.dot_general(
        owner.astype(F32), found, (((1,), (0,)), ((), ())), precision=lax.Precision.HIGHEST
    )
    maxima = jnp.sum(jnp.where(lane, lines, 0.0), axis=1)
    return (maxima, jnp.concatenate(centroids, axis=1))


def solution(mesh):
    placed = (P(("group", "rows"), None), P(("group", "rows")))
    return jax.shard_map(
        on_device,
        mesh=mesh,
        in_specs=placed,
        out_specs=(P(("group", "rows")), P(("group", "rows"), None)),
        check_vma=False,
    )
```

```python
import functools

import jax
import jax.numpy as jnp
from jax import lax
from jax.experimental import pallas as pl
from jax.experimental.pallas import tpu as pltpu
from jax.sharding import PartitionSpec as P

CLUSTERS = 256
LANES = 128
PIECES = 1
VMEM_LIMIT = 40 * 2**20
PARTS = ((3840, 256, 128), (0, 3840, 640))
F32 = jnp.float32
BF16 = jnp.bfloat16


def iota(shape, axis):
    return lax.broadcasted_iota(jnp.int32, shape, axis)


def mm(a, b):
    return lax.dot_general(a, b, (((1,), (0,)), ((), ())), preferred_element_type=F32)


def to_row(col):
    n = col.shape[0]
    return jnp.sum(jnp.where(iota((n, n), 0) == iota((n, n), 1), col, 0), axis=0, keepdims=True)


def to_col(row):
    n = row.shape[1]
    return jnp.sum(jnp.where(iota((n, n), 0) == iota((n, n), 1), row, 0), axis=1, keepdims=True)


def split(x):
    high = x.astype(BF16)
    return jnp.concatenate([high, (x - high.astype(F32)).astype(BF16)], axis=0)


def code_kernel(mark, core_ref, mine_ref, mate_ref, x_ref, y_ref, out_ref, pick0_ref, pick1_ref, num_ref):
    rows, tile = x_ref.shape
    core = core_ref[0]

    @pl.when(pl.program_id(0) == 0)
    def _():
        mine = mine_ref[...].reshape(1, rows)
        mate = mate_ref[...].reshape(1, rows)
        counts = []
        for k, pick_ref in enumerate((pick0_ref, pick1_ref)):
            ids = jnp.where(core == k, mine, mate)
            twin = (to_col(ids) == ids) & (iota((rows, rows), 0) < iota((rows, rows), 1))
            second = jnp.sum(twin.astype(F32), axis=0, keepdims=True) > 0.5
            member = iota((CLUSTERS, rows), 0) == ids
            upper = member & ~second if k == 0 else member
            for j in range(2):
                cols = slice(j * rows, (j + 1) * rows)
                pick_ref[:CLUSTERS, cols] = upper.astype(F32).astype(BF16)
                pick_ref[CLUSTERS:, cols] = (member & second).astype(F32).astype(BF16)
            counts.append(jnp.sum(member.astype(F32), axis=1, keepdims=True))
        num_ref[:CLUSTERS] = counts[0]
        num_ref[CLUSTERS : 2 * CLUSTERS] = counts[1]
        num_ref[2 * CLUSTERS :] = 1.0 / jnp.maximum(counts[0] + counts[1], 1.0)

    def body(x0_ref, x1_ref):
        rows0 = mm(pick0_ref[...], split(x0_ref[...]))
        rows1 = mm(pick1_ref[...], split(x1_ref[...]))
        count0 = num_ref[:CLUSTERS]
        count1 = num_ref[CLUSTERS : 2 * CLUSTERS]
        row0 = rows0[:CLUSTERS]
        row1 = rows0[CLUSTERS:]
        row3 = rows1[CLUSTERS:]
        mean = ((row0 + row1) + rows1[:CLUSTERS]) * num_ref[2 * CLUSTERS :]
        high = mean.astype(BF16)
        none = jnp.inf if mark else 0.0
        flag = jnp.where(count1 > 0.5, none, -none)
        out_ref[:, :tile] = jnp.where(count0 > 0.5, row0 - mean, none).astype(BF16)
        out_ref[:, tile : 2 * tile] = jnp.where(count0 > 1.5, row1 - mean, none).astype(BF16)
        out_ref[:, 2 * tile : 3 * tile] = jnp.where(count1 > 1.5, row3 - mean, flag).astype(BF16)
        out_ref[:, 3 * tile : 4 * tile] = high
        out_ref[:, 4 * tile :] = (mean - high.astype(F32)).astype(BF16)

    @pl.when(core == 0)
    def _():
        body(x_ref, y_ref)

    @pl.when(core == 1)
    def _():
        body(y_ref, x_ref)


def code(core, mine, mate, x, y, start, width, tile, mark):
    rows = x.shape[0]
    first = start // tile
    steps = width // 2 // tile
    line = pl.BlockSpec((rows,), lambda t, core: (0,))
    block = pl.BlockSpec((rows, tile), lambda t, core: (0, first + core[0] * steps + t))
    if y.shape[1] == tile:
        y = pltpu.with_memory_space_constraint(y, pltpu.VMEM)
        y_spec = pl.BlockSpec(memory_space=pltpu.VMEM)
    else:
        y_spec = block
    return pl.pallas_call(
        functools.partial(code_kernel, mark),
        grid_spec=pltpu.PrefetchScalarGridSpec(
            num_scalar_prefetch=1,
            grid=(steps,),
            in_specs=[line, pl.BlockSpec(memory_space=pltpu.VMEM), block, y_spec],
            out_specs=pl.BlockSpec((CLUSTERS, 5 * tile), lambda t, core: (0, t)),
            scratch_shapes=[
                pltpu.VMEM((2 * CLUSTERS, 2 * rows), BF16),
                pltpu.VMEM((2 * CLUSTERS, 2 * rows), BF16),
                pltpu.VMEM((3 * CLUSTERS, 1), F32),
            ],
        ),
        out_shape=jax.ShapeDtypeStruct((CLUSTERS, steps * 5 * tile), BF16),
    )(core, mine, pltpu.with_memory_space_constraint(mate, pltpu.VMEM), x, y)


def compare_kernel(cl_dev, width_all, pieces, first, last, *refs):
    refs = list(refs)
    got_refs = [refs.pop(0) for _ in range(pieces)]
    if not first:
        gram_in_ref, live_ref = refs.pop(0), refs.pop(0)
    centroid_refs = [refs.pop(0), refs.pop(0)]
    best_ref = refs.pop(0) if last else None
    gram_ref = refs.pop(0)
    if first:
        live_ref = refs.pop(0)
    count_ref, total_ref = refs
    slots = live_ref.shape[0] // 4
    tile = centroid_refs[0].shape[1]
    blocks = cl_dev % 8 == 0

    def part(core, lo, hi):
        found = [ref[:, core, :, lo:hi].astype(F32).reshape(-1, hi - lo) for ref in got_refs]
        return found[0] if pieces == 1 else jnp.concatenate(found, axis=0)

    @pl.when(pl.program_id(0) == 0)
    def _():
        gram_ref[...] = jnp.zeros_like(gram_ref) if first else gram_in_ref[...]
        if first:
            mark = part(0, 2 * tile, 2 * tile + LANES)[:, :1]
            live = [
                part(0, 0, LANES)[:, :1] < jnp.inf,
                part(0, tile, tile + LANES)[:, :1] < jnp.inf,
                mark > -jnp.inf,
                jnp.abs(mark) < jnp.inf,
            ]
            for k in range(4):
                live_ref[k * slots : (k + 1) * slots] = live[k].astype(F32)
        live = [live_ref[k * slots : (k + 1) * slots] for k in range(4)]
        count = live[0] + live[1] + live[2] + live[3]
        count_ref[...] = count
        same = (iota((slots, slots), 0) % cl_dev) == (iota((slots, slots), 1) % cl_dev)
        total_ref[...] = 1.0 / jnp.sum(jnp.where(same, to_row(count), 0.0), axis=1, keepdims=True)

    live = [live_ref[k * slots : (k + 1) * slots] > 0.5 for k in range(4)]
    count = count_ref[...]
    if not blocks:
        same = (iota((slots, slots), 0) % cl_dev) == (iota((slots, slots), 1) % cl_dev)
        mix = same.astype(F32)
    gram = gram_ref[...]
    for core in range(2):
        d0, d1, d3 = [part(core, k * tile, (k + 1) * tile) for k in range(3)]
        if first:
            d0 = jnp.where(live[0], d0, 0.0)
            d1 = jnp.where(live[1], d1, 0.0)
            d3 = jnp.where(live[3], d3, 0.0)
        mean = part(core, 3 * tile, 4 * tile) + part(core, 4 * tile, 5 * tile)
        if blocks:
            chips = slots // cl_dev
            sums = jnp.sum((mean * count).reshape(chips, cl_dev, tile), axis=0)
            centroid = sums * total_ref[:cl_dev]
            away = (mean.reshape(chips, cl_dev, tile) - centroid[None]).reshape(slots, tile)
        else:
            sums = lax.dot_general(
                mix,
                mean * count,
                (((1,), (0,)), ((), ())),
                precision=lax.Precision.HIGHEST,
                preferred_element_type=F32,
            )
            centroid = sums * total_ref[...]
            away = mean - centroid
        centroid_refs[core][...] = centroid[:cl_dev]
        rest = away - (d0 + d1 + d3)
        every = jnp.concatenate([away + d0, away + d1, rest, away + d3], axis=0).astype(BF16)
        gram += lax.dot_general(every, every, (((1,), (1,)), ((), ())), preferred_element_type=F32)
    gram_ref[...] = gram

    if last:

        @pl.when(pl.program_id(0) == pl.num_programs(0) - 1)
        def _():
            n = 4 * slots
            row = iota((n, n), 0)
            col = iota((n, n), 1)
            diag = jnp.where(row == col, gram, 0.0)
            inv_row = lax.rsqrt(jnp.sum(diag, axis=0, keepdims=True) / width_all + 1e-6)
            inv_col = lax.rsqrt(jnp.sum(diag, axis=1, keepdims=True) / width_all + 1e-6)
            score = gram * inv_col * inv_row / width_all
            usable = ((row % cl_dev) == (col % cl_dev)) & (row != col) & (live_ref[...] > 0.5)
            best = jnp.max(jnp.where(usable, score, -1.0), axis=0, keepdims=True)
            sources = 2 * slots // cl_dev
            place = iota((sources, n), 1)
            source = (place % slots) // cl_dev * 2 + place // (2 * slots)
            spread = jnp.where(source == iota((sources, n), 0), best, 0.0)
            place = iota((n, LANES), 0)
            lane = (place // slots) % 2 * cl_dev + place % cl_dev
            pick = (lane == iota((n, LANES), 1)).astype(F32)
            best_ref[...] = lax.dot_general(
                spread,
                pick,
                (((1,), (0,)), ((), ())),
                precision=lax.Precision.HIGHEST,
                preferred_element_type=F32,
            )


def compare(got, state, cl_dev, width_all, last, tile, resident):
    first = state is None
    slots = CLUSTERS // 2
    half = got.shape[1] // 5
    chips = slots // cl_dev
    got = got.reshape(chips, 2, cl_dev, got.shape[1])
    if cl_dev % 8:
        got = jnp.moveaxis(got, 1, 0).reshape(1, 2, slots, got.shape[3])
    fixed = lambda t: (0, 0)
    if resident:
        pieces = 1
        args = [pltpu.with_memory_space_constraint(got, pltpu.VMEM)]
        specs = [pl.BlockSpec(memory_space=pltpu.VMEM)]
    else:
        pieces = PIECES if cl_dev % 8 == 0 else 1
        args = [got] * pieces
        shape = (got.shape[0] // pieces, *got.shape[1:3], 5 * tile)
        specs = [pl.BlockSpec(shape, lambda t, k=k: (k, 0, 0, t)) for k in range(pieces)]
    square = jax.ShapeDtypeStruct((4 * slots, 4 * slots), F32)
    column = jax.ShapeDtypeStruct((4 * slots, 1), F32)
    square_spec = pl.BlockSpec(square.shape, fixed)
    column_spec = pl.BlockSpec(column.shape, fixed)
    out_shape = [jax.ShapeDtypeStruct((cl_dev, half), F32)] * 2
    out_specs = [pl.BlockSpec((cl_dev, tile), lambda t: (0, t))] * 2
    scratch = [pltpu.VMEM((slots, 1), F32)] * 2
    if last:
        out_shape.append(jax.ShapeDtypeStruct((2 * chips, LANES), F32))
        out_specs.append(pl.BlockSpec((2 * chips, LANES), fixed))
        scratch.insert(0, pltpu.VMEM(square.shape, F32))
    else:
        out_shape.append(square)
        out_specs.append(square_spec)
    if first:
        out_shape.append(column)
        out_specs.append(column_spec)
    else:
        args += [pltpu.with_memory_space_constraint(x, pltpu.VMEM) for x in state]
        specs += [pl.BlockSpec(memory_space=pltpu.VMEM)] * 2
    return pl.pallas_call(
        functools.partial(compare_kernel, cl_dev, width_all, pieces, first, last),
        grid=(half // tile,),
        in_specs=specs,
        out_specs=out_specs,
        out_shape=out_shape,
        scratch_shapes=scratch,
        compiler_params=pltpu.CompilerParams(vmem_limit_bytes=VMEM_LIMIT),
    )(*args)


def on_device(embeddings, assignment):
    dev_count = lax.axis_size("rows")
    cl_dev = CLUSTERS // dev_count
    rows, width = embeddings.shape
    core = lax.axis_index("rows") % 2
    exchange = functools.partial(lax.all_to_all, axis_name="rows", split_axis=0, concat_axis=0, tiled=True)
    swap = functools.partial(lax.ppermute, axis_name="rows", perm=[(i, i ^ 1) for i in range(dev_count)])
    mate = swap(assignment)
    first, part, _ = PARTS[0]
    half = part // 2
    head = swap(lax.dynamic_slice_in_dim(embeddings, first + (1 - core) * half, half, 1))
    whole, head, mate = lax.optimization_barrier((embeddings, head, mate))
    tail = swap(whole)
    got = []
    for start, part, tile in PARTS:
        coded = code(core.astype(jnp.int32).reshape(1), assignment, mate, embeddings, tail if got else head, start, part, tile, not got)
        coded, embeddings = lax.optimization_barrier((coded, embeddings))
        got.append(exchange(coded))
    c0, c1, *state = compare(got[0], None, cl_dev, width, False, PARTS[0][2], True)
    c2, c3, best = compare(got[1], state, cl_dev, width, True, PARTS[1][2], False)
    found = exchange(best)
    row_ids = jnp.arange(rows, dtype=jnp.int32)
    twin = (assignment[:, None] == assignment[None, :]) & (row_ids[None, :] < row_ids[:, None])
    second = jnp.sum(twin.astype(jnp.int32), axis=1)
    owner = (assignment // cl_dev)[:, None] == jnp.arange(dev_count, dtype=jnp.int32)[None, :]
    lane = (second * cl_dev + assignment % cl_dev)[:, None] == jnp.arange(LANES, dtype=jnp.int32)[None, :]
    lines = lax.dot_general(
        owner.astype(F32), found, (((1,), (0,)), ((), ())), precision=lax.Precision.HIGHEST
    )
    maxima = jnp.sum(jnp.where(lane, lines, 0.0), axis=1)
    return (maxima, jnp.concatenate([c2, c3, c0, c1], axis=1))


def solution(mesh):
    placed = (P(("group", "rows"), None), P(("group", "rows")))
    return jax.shard_map(
        on_device,
        mesh=mesh,
        in_specs=placed,
        out_specs=(P(("group", "rows")), P(("group", "rows"), None)),
        check_vma=False,
    )
```

```python
import functools

import jax
import jax.numpy as jnp
from jax import lax
from jax.experimental import pallas as pl
from jax.experimental.pallas import tpu as pltpu
from jax.sharding import PartitionSpec as P

CLUSTERS = 256
LANES = 128
VMEM_LIMIT = 40 * 2**20
PARTS = ((3840, 256, 128), (0, 3840, 640))
F32 = jnp.float32
BF16 = jnp.bfloat16


def iota(shape, axis):
    return lax.broadcasted_iota(jnp.int32, shape, axis)


def mm(a, b):
    return lax.dot_general(a, b, (((1,), (0,)), ((), ())), preferred_element_type=F32)


def to_row(col):
    n = col.shape[0]
    return jnp.sum(jnp.where(iota((n, n), 0) == iota((n, n), 1), col, 0), axis=0, keepdims=True)


def to_col(row):
    n = row.shape[1]
    return jnp.sum(jnp.where(iota((n, n), 0) == iota((n, n), 1), row, 0), axis=1, keepdims=True)


def split(x):
    high = x.astype(BF16)
    return jnp.concatenate([high, (x - high.astype(F32)).astype(BF16)], axis=0)


def code_kernel(mark, core_ref, mine_ref, mate_ref, x_ref, y_ref, out_ref, pick0_ref, pick1_ref, num_ref):
    rows, tile = x_ref.shape
    core = core_ref[0]

    @pl.when(pl.program_id(0) == 0)
    def _():
        mine = mine_ref[...].reshape(1, rows)
        mate = mate_ref[...].reshape(1, rows)
        counts = []
        for k, pick_ref in enumerate((pick0_ref, pick1_ref)):
            ids = jnp.where(core == k, mine, mate)
            twin = (to_col(ids) == ids) & (iota((rows, rows), 0) < iota((rows, rows), 1))
            second = jnp.sum(twin.astype(F32), axis=0, keepdims=True) > 0.5
            member = iota((CLUSTERS, rows), 0) == ids
            upper = member & ~second if k == 0 else member
            for j in range(2):
                cols = slice(j * rows, (j + 1) * rows)
                pick_ref[:CLUSTERS, cols] = upper.astype(F32).astype(BF16)
                pick_ref[CLUSTERS:, cols] = (member & second).astype(F32).astype(BF16)
            counts.append(jnp.sum(member.astype(F32), axis=1, keepdims=True))
        num_ref[:CLUSTERS] = counts[0]
        num_ref[CLUSTERS : 2 * CLUSTERS] = counts[1]
        num_ref[2 * CLUSTERS :] = 1.0 / jnp.maximum(counts[0] + counts[1], 1.0)

    def body(x0_ref, x1_ref):
        rows0 = mm(pick0_ref[...], split(x0_ref[...]))
        rows1 = mm(pick1_ref[...], split(x1_ref[...]))
        count0 = num_ref[:CLUSTERS]
        count1 = num_ref[CLUSTERS : 2 * CLUSTERS]
        row0 = rows0[:CLUSTERS]
        row1 = rows0[CLUSTERS:]
        row3 = rows1[CLUSTERS:]
        mean = ((row0 + row1) + rows1[:CLUSTERS]) * num_ref[2 * CLUSTERS :]
        high = mean.astype(BF16)
        none = jnp.inf if mark else 0.0
        flag = jnp.where(count1 > 0.5, none, -none)
        out_ref[:, :tile] = jnp.where(count0 > 0.5, row0 - mean, none).astype(BF16)
        out_ref[:, tile : 2 * tile] = jnp.where(count0 > 1.5, row1 - mean, none).astype(BF16)
        out_ref[:, 2 * tile : 3 * tile] = jnp.where(count1 > 1.5, row3 - mean, flag).astype(BF16)
        out_ref[:, 3 * tile : 4 * tile] = high
        out_ref[:, 4 * tile :] = (mean - high.astype(F32)).astype(BF16)

    @pl.when(core == 0)
    def _():
        body(x_ref, y_ref)

    @pl.when(core == 1)
    def _():
        body(y_ref, x_ref)


def code(core, mine, mate, x, y, start, width, tile, mark):
    rows = x.shape[0]
    first = start // tile
    steps = width // 2 // tile
    line = pl.BlockSpec((rows,), lambda t, core: (0,))
    block = pl.BlockSpec((rows, tile), lambda t, core: (0, first + core[0] * steps + t))
    if y.shape[1] == tile:
        y = pltpu.with_memory_space_constraint(y, pltpu.VMEM)
        y_spec = pl.BlockSpec(memory_space=pltpu.VMEM)
    else:
        y_spec = block
    return pl.pallas_call(
        functools.partial(code_kernel, mark),
        grid_spec=pltpu.PrefetchScalarGridSpec(
            num_scalar_prefetch=1,
            grid=(steps,),
            in_specs=[line, pl.BlockSpec(memory_space=pltpu.VMEM), block, y_spec],
            out_specs=pl.BlockSpec((CLUSTERS, 5 * tile), lambda t, core: (0, t)),
            scratch_shapes=[
                pltpu.VMEM((2 * CLUSTERS, 2 * rows), BF16),
                pltpu.VMEM((2 * CLUSTERS, 2 * rows), BF16),
                pltpu.VMEM((3 * CLUSTERS, 1), F32),
            ],
        ),
        out_shape=jax.ShapeDtypeStruct((CLUSTERS, steps * 5 * tile), BF16),
    )(core, mine, pltpu.with_memory_space_constraint(mate, pltpu.VMEM), x, y)


def compare_kernel(cl_dev, width_all, tile, first, *refs):
    if first:
        got_ref, *centroid_refs, gram_ref, live_ref = refs
        slots = CLUSTERS // 2
        buffers = [got_ref]
    else:
        got_ref, gram_in_ref, live_ref, *centroid_refs, best_ref, gram_ref, buf_ref, sems = refs
        slots = live_ref.shape[0] // 4
        buffers = [buf_ref.at[t] for t in range(buf_ref.shape[0])]
        copies = [
            pltpu.make_async_copy(got_ref.at[:, :, :, t * 5 * tile : (t + 1) * 5 * tile], buffer, sems.at[t])
            for t, buffer in enumerate(buffers)
        ]
        for copy in copies:
            copy.start()

    def part(buffer, core, k):
        return buffer[:, core, :, k * tile : (k + 1) * tile].astype(F32).reshape(slots, tile)

    if first:
        mark = part(got_ref, 0, 2)[:, :1]
        live = [
            part(got_ref, 0, 0)[:, :1] < jnp.inf,
            part(got_ref, 0, 1)[:, :1] < jnp.inf,
            mark > -jnp.inf,
            jnp.abs(mark) < jnp.inf,
        ]
        for k in range(4):
            live_ref[k * slots : (k + 1) * slots] = live[k].astype(F32)
    alive = [live_ref[k * slots : (k + 1) * slots] for k in range(4)]
    count = alive[0] + alive[1] + alive[2] + alive[3]
    same = (iota((slots, slots), 0) % cl_dev) == (iota((slots, slots), 1) % cl_dev)
    scale = 1.0 / jnp.sum(jnp.where(same, to_row(count), 0.0), axis=1, keepdims=True)
    half = 2 * slots
    for t, buffer in enumerate(buffers):
        if not first:
            copies[t].wait()
        rows = []
        for core in range(2):
            d0, d1, d3 = [part(buffer, core, k) for k in range(3)]
            if first:
                d0 = jnp.where(live[0], d0, 0.0)
                d1 = jnp.where(live[1], d1, 0.0)
                d3 = jnp.where(live[3], d3, 0.0)
            mean = part(buffer, core, 3) + part(buffer, core, 4)
            if cl_dev % 8 == 0:
                chips = slots // cl_dev
                centroid = jnp.sum((mean * count).reshape(chips, cl_dev, tile), axis=0) * scale[:cl_dev]
                away = (mean.reshape(chips, cl_dev, tile) - centroid[None]).reshape(slots, tile)
            else:
                sums = lax.dot_general(
                    same.astype(F32),
                    mean * count,
                    (((1,), (0,)), ((), ())),
                    precision=lax.Precision.HIGHEST,
                    preferred_element_type=F32,
                )
                centroid = sums * scale
                away = mean - centroid
            centroid_refs[core][:, t * tile : (t + 1) * tile] = centroid[:cl_dev]
            rest = away - (d0 + d1 + d3)
            rows.append(jnp.concatenate([away + d0, away + d1, rest, away + d3], axis=0).astype(BF16))
        every = jnp.concatenate(rows, axis=1)
        upper = lax.dot_general(every[:half], every, (((1,), (1,)), ((), ())), preferred_element_type=F32)
        lower = lax.dot_general(every[half:], every[half:], (((1,), (1,)), ((), ())), preferred_element_type=F32)
        if first:
            gram_ref[:half] = upper
            gram_ref[half:, half:] = lower
            gram_ref[half:, :half] = jnp.zeros((half, half), F32)
        else:
            old_ref = gram_ref if t else gram_in_ref
            gram_ref[:half] = old_ref[:half] + upper
            gram_ref[half:, half:] = old_ref[half:, half:] + lower

    if not first:
        gram_ref[half:, :half] = jnp.transpose(gram_ref[:half, half:])
        n = 4 * slots
        gram = gram_ref[...]
        row = iota((n, n), 0)
        col = iota((n, n), 1)
        diag = jnp.where(row == col, gram, 0.0)
        inv_row = lax.rsqrt(jnp.sum(diag, axis=0, keepdims=True) / width_all + 1e-6)
        inv_col = lax.rsqrt(jnp.sum(diag, axis=1, keepdims=True) / width_all + 1e-6)
        score = gram * inv_col * inv_row / width_all
        usable = ((row % cl_dev) == (col % cl_dev)) & (row != col) & (live_ref[...] > 0.5)
        best = jnp.max(jnp.where(usable, score, -1.0), axis=0, keepdims=True)
        sources = 2 * slots // cl_dev
        place = iota((sources, n), 1)
        source = (place % slots) // cl_dev * 2 + place // (2 * slots)
        spread = jnp.where(source == iota((sources, n), 0), best, 0.0)
        place = iota((n, LANES), 0)
        lane = (place // slots) % 2 * cl_dev + place % cl_dev
        pick = (lane == iota((n, LANES), 1)).astype(F32)
        best_ref[...] = lax.dot_general(
            spread,
            pick,
            (((1,), (0,)), ((), ())),
            precision=lax.Precision.HIGHEST,
            preferred_element_type=F32,
        )


def compare(got, state, cl_dev, width_all, tile):
    first = state is None
    slots = CLUSTERS // 2
    half = got.shape[1] // 5
    chips = slots // cl_dev
    got = got.reshape(chips, 2, cl_dev, got.shape[1])
    if cl_dev % 8:
        got = jnp.moveaxis(got, 1, 0).reshape(1, 2, slots, got.shape[3])
    near = lambda x: pltpu.with_memory_space_constraint(x, pltpu.VMEM)
    vmem = pl.BlockSpec(memory_space=pltpu.VMEM)
    square = jax.ShapeDtypeStruct((4 * slots, 4 * slots), F32)
    out_shape = [jax.ShapeDtypeStruct((cl_dev, half), F32)] * 2
    if first:
        args = [near(got)]
        specs = [vmem]
        out_shape += [square, jax.ShapeDtypeStruct((4 * slots, 1), F32)]
        scratch = []
    else:
        args = [got] + [near(x) for x in state]
        specs = [pl.BlockSpec(memory_space=pl.ANY), vmem, vmem]
        out_shape.append(jax.ShapeDtypeStruct((2 * chips, LANES), F32))
        steps = half // tile
        scratch = [
            pltpu.VMEM(square.shape, F32),
            pltpu.VMEM((steps, *got.shape[:3], 5 * tile), BF16),
            pltpu.SemaphoreType.DMA((steps,)),
        ]
    return pl.pallas_call(
        functools.partial(compare_kernel, cl_dev, width_all, tile, first),
        in_specs=specs,
        out_specs=[vmem] * len(out_shape),
        out_shape=out_shape,
        scratch_shapes=scratch,
        compiler_params=pltpu.CompilerParams(vmem_limit_bytes=VMEM_LIMIT),
    )(*args)


def on_device(embeddings, assignment):
    dev_count = lax.axis_size("rows")
    cl_dev = CLUSTERS // dev_count
    rows, width = embeddings.shape
    core = lax.axis_index("rows") % 2
    exchange = functools.partial(lax.all_to_all, axis_name="rows", split_axis=0, concat_axis=0, tiled=True)
    swap = functools.partial(lax.ppermute, axis_name="rows", perm=[(i, i ^ 1) for i in range(dev_count)])
    mate = swap(assignment)
    first, part, _ = PARTS[0]
    half = part // 2
    head = swap(lax.dynamic_slice_in_dim(embeddings, first + (1 - core) * half, half, 1))
    whole, head, mate = lax.optimization_barrier((embeddings, head, mate))
    tail = swap(whole)
    got = []
    for start, part, tile in PARTS:
        coded = code(core.astype(jnp.int32).reshape(1), assignment, mate, embeddings, tail if got else head, start, part, tile, not got)
        coded, embeddings = lax.optimization_barrier((coded, embeddings))
        got.append(exchange(coded))
    c0, c1, *state = compare(got[0], None, cl_dev, width, PARTS[0][2])
    c2, c3, best = compare(got[1], state, cl_dev, width, PARTS[1][2])
    found = exchange(best)
    row_ids = jnp.arange(rows, dtype=jnp.int32)
    twin = (assignment[:, None] == assignment[None, :]) & (row_ids[None, :] < row_ids[:, None])
    second = jnp.sum(twin.astype(jnp.int32), axis=1)
    owner = (assignment // cl_dev)[:, None] == jnp.arange(dev_count, dtype=jnp.int32)[None, :]
    lane = (second * cl_dev + assignment % cl_dev)[:, None] == jnp.arange(LANES, dtype=jnp.int32)[None, :]
    lines = lax.dot_general(
        owner.astype(F32), found, (((1,), (0,)), ((), ())), precision=lax.Precision.HIGHEST
    )
    maxima = jnp.sum(jnp.where(lane, lines, 0.0), axis=1)
    return (maxima, jnp.concatenate([c2, c3, c0, c1], axis=1))


def solution(mesh):
    placed = (P(("group", "rows"), None), P(("group", "rows")))
    return jax.shard_map(
        on_device,
        mesh=mesh,
        in_specs=placed,
        out_specs=(P(("group", "rows")), P(("group", "rows"), None)),
        check_vma=False,
    )
```

```python
import functools

import jax
import jax.numpy as jnp
from jax import lax
from jax.experimental import pallas as pl
from jax.experimental.pallas import tpu as pltpu
from jax.sharding import PartitionSpec as P

CLUSTERS = 256
LANES = 128
VMEM_LIMIT = 40 * 2**20
PARTS = ((3584, 512, 256), (0, 3584, 896))
F32 = jnp.float32
BF16 = jnp.bfloat16


def iota(shape, axis):
    return lax.broadcasted_iota(jnp.int32, shape, axis)


def mm(a, b):
    return lax.dot_general(a, b, (((1,), (0,)), ((), ())), preferred_element_type=F32)


def to_row(col):
    n = col.shape[0]
    return jnp.sum(jnp.where(iota((n, n), 0) == iota((n, n), 1), col, 0), axis=0, keepdims=True)


def to_col(row):
    n = row.shape[1]
    return jnp.sum(jnp.where(iota((n, n), 0) == iota((n, n), 1), row, 0), axis=1, keepdims=True)


def split(x):
    high = x.astype(BF16)
    return jnp.concatenate([high, (x - high.astype(F32)).astype(BF16)], axis=0)


def code_kernel(mark, core_ref, mine_ref, mate_ref, x_ref, y_ref, out_ref, pick0_ref, pick1_ref, num_ref):
    rows, tile = x_ref.shape
    core = core_ref[0]

    @pl.when(pl.program_id(0) == 0)
    def _():
        mine = mine_ref[...].reshape(1, rows)
        mate = mate_ref[...].reshape(1, rows)
        counts = []
        for k, pick_ref in enumerate((pick0_ref, pick1_ref)):
            ids = jnp.where(core == k, mine, mate)
            twin = (to_col(ids) == ids) & (iota((rows, rows), 0) < iota((rows, rows), 1))
            second = jnp.sum(twin.astype(F32), axis=0, keepdims=True) > 0.5
            member = iota((CLUSTERS, rows), 0) == ids
            upper = member & ~second if k == 0 else member
            for j in range(2):
                cols = slice(j * rows, (j + 1) * rows)
                pick_ref[:CLUSTERS, cols] = upper.astype(F32).astype(BF16)
                pick_ref[CLUSTERS:, cols] = (member & second).astype(F32).astype(BF16)
            counts.append(jnp.sum(member.astype(F32), axis=1, keepdims=True))
        num_ref[:CLUSTERS] = counts[0]
        num_ref[CLUSTERS : 2 * CLUSTERS] = counts[1]
        num_ref[2 * CLUSTERS :] = 1.0 / jnp.maximum(counts[0] + counts[1], 1.0)

    def body(x0_ref, x1_ref):
        rows0 = mm(pick0_ref[...], split(x0_ref[...]))
        rows1 = mm(pick1_ref[...], split(x1_ref[...]))
        count0 = num_ref[:CLUSTERS]
        count1 = num_ref[CLUSTERS : 2 * CLUSTERS]
        row0 = rows0[:CLUSTERS]
        row1 = rows0[CLUSTERS:]
        row3 = rows1[CLUSTERS:]
        mean = ((row0 + row1) + rows1[:CLUSTERS]) * num_ref[2 * CLUSTERS :]
        high = mean.astype(BF16)
        none = jnp.inf if mark else 0.0
        flag = jnp.where(count1 > 0.5, none, -none)
        out_ref[:, :tile] = jnp.where(count0 > 0.5, row0 - mean, none).astype(BF16)
        out_ref[:, tile : 2 * tile] = jnp.where(count0 > 1.5, row1 - mean, none).astype(BF16)
        out_ref[:, 2 * tile : 3 * tile] = jnp.where(count1 > 1.5, row3 - mean, flag).astype(BF16)
        out_ref[:, 3 * tile : 4 * tile] = high
        out_ref[:, 4 * tile :] = (mean - high.astype(F32)).astype(BF16)

    @pl.when(core == 0)
    def _():
        body(x_ref, y_ref)

    @pl.when(core == 1)
    def _():
        body(y_ref, x_ref)


def code(core, mine, mate, x, y, start, width, tile, mark):
    rows = x.shape[0]
    first = start // tile
    steps = width // 2 // tile
    line = pl.BlockSpec((rows,), lambda t, core: (0,))
    block = pl.BlockSpec((rows, tile), lambda t, core: (0, first + core[0] * steps + t))
    if y.shape[1] == tile:
        y = pltpu.with_memory_space_constraint(y, pltpu.VMEM)
        y_spec = pl.BlockSpec(memory_space=pltpu.VMEM)
    else:
        y_spec = block
    return pl.pallas_call(
        functools.partial(code_kernel, mark),
        grid_spec=pltpu.PrefetchScalarGridSpec(
            num_scalar_prefetch=1,
            grid=(steps,),
            in_specs=[line, pl.BlockSpec(memory_space=pltpu.VMEM), block, y_spec],
            out_specs=pl.BlockSpec((CLUSTERS, 5 * tile), lambda t, core: (0, t)),
            scratch_shapes=[
                pltpu.VMEM((2 * CLUSTERS, 2 * rows), BF16),
                pltpu.VMEM((2 * CLUSTERS, 2 * rows), BF16),
                pltpu.VMEM((3 * CLUSTERS, 1), F32),
            ],
        ),
        out_shape=jax.ShapeDtypeStruct((CLUSTERS, steps * 5 * tile), BF16),
    )(core, mine, pltpu.with_memory_space_constraint(mate, pltpu.VMEM), x, y)


def compare_kernel(cl_dev, width_all, tile, first, *refs):
    if first:
        got_ref, *centroid_refs, gram_ref, live_ref = refs
        slots = CLUSTERS // 2
        buffers = [got_ref]
    else:
        got_ref, gram_in_ref, live_ref, *centroid_refs, best_ref, gram_ref, buf_ref, sems = refs
        slots = live_ref.shape[0] // 4
        buffers = [buf_ref.at[t] for t in range(buf_ref.shape[0])]
        copies = [
            pltpu.make_async_copy(got_ref.at[:, :, :, t * 5 * tile : (t + 1) * 5 * tile], buffer, sems.at[t])
            for t, buffer in enumerate(buffers)
        ]
        for copy in copies:
            copy.start()

    def part(buffer, core, k):
        return buffer[:, core, :, k * tile : (k + 1) * tile].astype(F32).reshape(slots, tile)

    if first:
        mark = part(got_ref, 0, 2)[:, :1]
        live = [
            part(got_ref, 0, 0)[:, :1] < jnp.inf,
            part(got_ref, 0, 1)[:, :1] < jnp.inf,
            mark > -jnp.inf,
            jnp.abs(mark) < jnp.inf,
        ]
        for k in range(4):
            live_ref[k * slots : (k + 1) * slots] = live[k].astype(F32)
    alive = [live_ref[k * slots : (k + 1) * slots] for k in range(4)]
    count = alive[0] + alive[1] + alive[2] + alive[3]
    same = (iota((slots, slots), 0) % cl_dev) == (iota((slots, slots), 1) % cl_dev)
    scale = 1.0 / jnp.sum(jnp.where(same, to_row(count), 0.0), axis=1, keepdims=True)
    half = 2 * slots
    for t, buffer in enumerate(buffers):
        if not first:
            copies[t].wait()
        rows = []
        for core in range(2):
            d0, d1, d3 = [part(buffer, core, k) for k in range(3)]
            if first:
                d0 = jnp.where(live[0], d0, 0.0)
                d1 = jnp.where(live[1], d1, 0.0)
                d3 = jnp.where(live[3], d3, 0.0)
            mean = part(buffer, core, 3) + part(buffer, core, 4)
            if cl_dev % 8 == 0:
                chips = slots // cl_dev
                centroid = jnp.sum((mean * count).reshape(chips, cl_dev, tile), axis=0) * scale[:cl_dev]
                away = (mean.reshape(chips, cl_dev, tile) - centroid[None]).reshape(slots, tile)
            else:
                sums = lax.dot_general(
                    same.astype(F32),
                    mean * count,
                    (((1,), (0,)), ((), ())),
                    precision=lax.Precision.HIGHEST,
                    preferred_element_type=F32,
                )
                centroid = sums * scale
                away = mean - centroid
            centroid_refs[core][:, t * tile : (t + 1) * tile] = centroid[:cl_dev]
            rest = away - (d0 + d1 + d3)
            rows.append(jnp.concatenate([away + d0, away + d1, rest, away + d3], axis=0).astype(BF16))
        every = jnp.concatenate(rows, axis=1)
        upper = lax.dot_general(every[:half], every, (((1,), (1,)), ((), ())), preferred_element_type=F32)
        lower = lax.dot_general(every[half:], every[half:], (((1,), (1,)), ((), ())), preferred_element_type=F32)
        if first:
            gram_ref[:half] = upper
            gram_ref[half:, half:] = lower
            gram_ref[half:, :half] = jnp.zeros((half, half), F32)
        else:
            old_ref = gram_ref if t else gram_in_ref
            gram_ref[:half] = old_ref[:half] + upper
            gram_ref[half:, half:] = old_ref[half:, half:] + lower

    if not first:
        gram_ref[half:, :half] = jnp.transpose(gram_ref[:half, half:])
        n = 4 * slots
        gram = gram_ref[...]
        row = iota((n, n), 0)
        col = iota((n, n), 1)
        diag = jnp.where(row == col, gram, 0.0)
        inv_row = lax.rsqrt(jnp.sum(diag, axis=0, keepdims=True) / width_all + 1e-6)
        inv_col = lax.rsqrt(jnp.sum(diag, axis=1, keepdims=True) / width_all + 1e-6)
        score = gram * inv_col * inv_row / width_all
        usable = ((row % cl_dev) == (col % cl_dev)) & (row != col) & (live_ref[...] > 0.5)
        best = jnp.max(jnp.where(usable, score, -1.0), axis=0, keepdims=True)
        sources = 2 * slots // cl_dev
        place = iota((sources, n), 1)
        source = (place % slots) // cl_dev * 2 + place // (2 * slots)
        spread = jnp.where(source == iota((sources, n), 0), best, 0.0)
        place = iota((n, LANES), 0)
        lane = (place // slots) % 2 * cl_dev + place % cl_dev
        pick = (lane == iota((n, LANES), 1)).astype(F32)
        best_ref[...] = lax.dot_general(
            spread,
            pick,
            (((1,), (0,)), ((), ())),
            precision=lax.Precision.HIGHEST,
            preferred_element_type=F32,
        )


def compare(got, state, cl_dev, width_all, tile):
    first = state is None
    slots = CLUSTERS // 2
    half = got.shape[1] // 5
    chips = slots // cl_dev
    got = got.reshape(chips, 2, cl_dev, got.shape[1])
    if cl_dev % 8:
        got = jnp.moveaxis(got, 1, 0).reshape(1, 2, slots, got.shape[3])
    near = lambda x: pltpu.with_memory_space_constraint(x, pltpu.VMEM)
    vmem = pl.BlockSpec(memory_space=pltpu.VMEM)
    square = jax.ShapeDtypeStruct((4 * slots, 4 * slots), F32)
    out_shape = [jax.ShapeDtypeStruct((cl_dev, half), F32)] * 2
    if first:
        args = [near(got)]
        specs = [vmem]
        out_shape += [square, jax.ShapeDtypeStruct((4 * slots, 1), F32)]
        scratch = []
    else:
        args = [got] + [near(x) for x in state]
        specs = [pl.BlockSpec(memory_space=pl.ANY), vmem, vmem]
        out_shape.append(jax.ShapeDtypeStruct((2 * chips, LANES), F32))
        steps = half // tile
        scratch = [
            pltpu.VMEM(square.shape, F32),
            pltpu.VMEM((steps, *got.shape[:3], 5 * tile), BF16),
            pltpu.SemaphoreType.DMA((steps,)),
        ]
    return pl.pallas_call(
        functools.partial(compare_kernel, cl_dev, width_all, tile, first),
        in_specs=specs,
        out_specs=[vmem] * len(out_shape),
        out_shape=out_shape,
        scratch_shapes=scratch,
        compiler_params=pltpu.CompilerParams(vmem_limit_bytes=VMEM_LIMIT),
    )(*args)


def on_device(embeddings, assignment):
    dev_count = lax.axis_size("rows")
    cl_dev = CLUSTERS // dev_count
    rows, width = embeddings.shape
    core = lax.axis_index("rows") % 2
    exchange = functools.partial(lax.all_to_all, axis_name="rows", split_axis=0, concat_axis=0, tiled=True)
    swap = functools.partial(lax.ppermute, axis_name="rows", perm=[(i, i ^ 1) for i in range(dev_count)])
    mate = swap(assignment)
    first, part, _ = PARTS[0]
    half = part // 2
    head = swap(lax.dynamic_slice_in_dim(embeddings, first + (1 - core) * half, half, 1))
    whole, head, mate = lax.optimization_barrier((embeddings, head, mate))
    tail = swap(whole)
    got = []
    for start, part, tile in PARTS:
        coded = code(core.astype(jnp.int32).reshape(1), assignment, mate, embeddings, tail if got else head, start, part, tile, not got)
        coded, embeddings = lax.optimization_barrier((coded, embeddings))
        got.append(exchange(coded))
    c0, c1, *state = compare(got[0], None, cl_dev, width, PARTS[0][2])
    c2, c3, best = compare(got[1], state, cl_dev, width, PARTS[1][2])
    found = exchange(best)
    row_ids = jnp.arange(rows, dtype=jnp.int32)
    twin = (assignment[:, None] == assignment[None, :]) & (row_ids[None, :] < row_ids[:, None])
    second = jnp.sum(twin.astype(jnp.int32), axis=1)
    owner = (assignment // cl_dev)[:, None] == jnp.arange(dev_count, dtype=jnp.int32)[None, :]
    lane = (second * cl_dev + assignment % cl_dev)[:, None] == jnp.arange(LANES, dtype=jnp.int32)[None, :]
    lines = lax.dot_general(
        owner.astype(F32), found, (((1,), (0,)), ((), ())), precision=lax.Precision.HIGHEST
    )
    maxima = jnp.sum(jnp.where(lane, lines, 0.0), axis=1)
    return (maxima, jnp.concatenate([c2, c3, c0, c1], axis=1))


def solution(mesh):
    placed = (P(("group", "rows"), None), P(("group", "rows")))
    return jax.shard_map(
        on_device,
        mesh=mesh,
        in_specs=placed,
        out_specs=(P(("group", "rows")), P(("group", "rows"), None)),
        check_vma=False,
    )
```

```python
import functools

import jax
import jax.numpy as jnp
from jax import lax
from jax.experimental import pallas as pl
from jax.experimental.pallas import tpu as pltpu
from jax.sharding import PartitionSpec as P

CLUSTERS = 256
LANES = 128
VMEM_LIMIT = 40 * 2**20
PARTS = ((3584, 512, 256), (0, 3584, 896))
F32 = jnp.float32
BF16 = jnp.bfloat16


def iota(shape, axis):
    return lax.broadcasted_iota(jnp.int32, shape, axis)


def mm(a, b):
    return lax.dot_general(a, b, (((1,), (0,)), ((), ())), preferred_element_type=F32)


def to_row(col):
    n = col.shape[0]
    return jnp.sum(jnp.where(iota((n, n), 0) == iota((n, n), 1), col, 0), axis=0, keepdims=True)


def to_col(row):
    n = row.shape[1]
    return jnp.sum(jnp.where(iota((n, n), 0) == iota((n, n), 1), row, 0), axis=1, keepdims=True)


def split(x):
    high = x.astype(BF16)
    return jnp.concatenate([high, (x - high.astype(F32)).astype(BF16)], axis=0)


def code_kernel(mark, core_ref, mine_ref, mate_ref, x_ref, y_ref, out_ref, pick0_ref, pick1_ref, num_ref):
    rows, tile = x_ref.shape
    core = core_ref[0]

    @pl.when(pl.program_id(0) == 0)
    def _():
        mine = mine_ref[...].reshape(1, rows)
        mate = mate_ref[...].reshape(1, rows)
        before = (iota((rows, 1), 0) < iota((1, rows), 1)).astype(F32).astype(BF16)
        counts = []
        for k, pick_ref in enumerate((pick0_ref, pick1_ref)):
            member = iota((CLUSTERS, 1), 0) == jnp.where(core == k, mine, mate)
            marks = member.astype(F32)
            rank = mm(marks.astype(BF16), before)
            second = jnp.where(member, rank, 0.0)
            upper = (marks - second if k == 0 else marks).astype(BF16)
            second = second.astype(BF16)
            for j in range(2):
                cols = slice(j * rows, (j + 1) * rows)
                pick_ref[:CLUSTERS, cols] = upper
                pick_ref[CLUSTERS:, cols] = second
            counts.append(jnp.sum(marks, axis=1, keepdims=True))
        num_ref[:CLUSTERS] = counts[0]
        num_ref[CLUSTERS : 2 * CLUSTERS] = counts[1]
        num_ref[2 * CLUSTERS :] = 1.0 / jnp.maximum(counts[0] + counts[1], 1.0)

    def body(x0_ref, x1_ref):
        rows0 = mm(pick0_ref[...], split(x0_ref[...]))
        rows1 = mm(pick1_ref[...], split(x1_ref[...]))
        count0 = num_ref[:CLUSTERS]
        count1 = num_ref[CLUSTERS : 2 * CLUSTERS]
        row0 = rows0[:CLUSTERS]
        row1 = rows0[CLUSTERS:]
        row3 = rows1[CLUSTERS:]
        mean = ((row0 + row1) + rows1[:CLUSTERS]) * num_ref[2 * CLUSTERS :]
        high = mean.astype(BF16)
        none = jnp.inf if mark else 0.0
        flag = jnp.where(count1 > 0.5, none, -none)
        out_ref[:, :tile] = jnp.where(count0 > 0.5, row0 - mean, none).astype(BF16)
        out_ref[:, tile : 2 * tile] = jnp.where(count0 > 1.5, row1 - mean, none).astype(BF16)
        out_ref[:, 2 * tile : 3 * tile] = jnp.where(count1 > 1.5, row3 - mean, flag).astype(BF16)
        out_ref[:, 3 * tile : 4 * tile] = high
        out_ref[:, 4 * tile :] = (mean - high.astype(F32)).astype(BF16)

    @pl.when(core == 0)
    def _():
        body(x_ref, y_ref)

    @pl.when(core == 1)
    def _():
        body(y_ref, x_ref)


def code(core, mine, mate, x, y, start, width, tile, mark):
    rows = x.shape[0]
    first = start // tile
    steps = width // 2 // tile
    line = pl.BlockSpec((rows,), lambda t, core: (0,))
    block = pl.BlockSpec((rows, tile), lambda t, core: (0, first + core[0] * steps + t))
    if y.shape[1] == tile:
        x, y = [pltpu.with_memory_space_constraint(z, pltpu.VMEM) for z in (x, y)]
        block = pl.BlockSpec(memory_space=pltpu.VMEM)
    return pl.pallas_call(
        functools.partial(code_kernel, mark),
        grid_spec=pltpu.PrefetchScalarGridSpec(
            num_scalar_prefetch=1,
            grid=(steps,),
            in_specs=[line, pl.BlockSpec(memory_space=pltpu.VMEM), block, block],
            out_specs=pl.BlockSpec((CLUSTERS, 5 * tile), lambda t, core: (0, t)),
            scratch_shapes=[
                pltpu.VMEM((2 * CLUSTERS, 2 * rows), BF16),
                pltpu.VMEM((2 * CLUSTERS, 2 * rows), BF16),
                pltpu.VMEM((3 * CLUSTERS, 1), F32),
            ],
        ),
        out_shape=jax.ShapeDtypeStruct((CLUSTERS, steps * 5 * tile), BF16),
    )(core, mine, pltpu.with_memory_space_constraint(mate, pltpu.VMEM), x, y)


def compare_kernel(cl_dev, width_all, tile, first, *refs):
    if first:
        got_ref, *centroid_refs, gram_ref, live_ref = refs
        slots = CLUSTERS // 2
        buffers = [got_ref]
    else:
        got_ref, gram_in_ref, live_ref, *centroid_refs, best_ref, gram_ref, buf_ref, sems = refs
        slots = live_ref.shape[0] // 4
        buffers = [buf_ref.at[t] for t in range(buf_ref.shape[0])]
        copies = [
            pltpu.make_async_copy(got_ref.at[:, :, :, t * 5 * tile : (t + 1) * 5 * tile], buffer, sems.at[t])
            for t, buffer in enumerate(buffers)
        ]
        for copy in copies:
            copy.start()

    def part(buffer, core, k):
        return buffer[:, core, :, k * tile : (k + 1) * tile].astype(F32).reshape(slots, tile)

    if first:
        mark = part(got_ref, 0, 2)[:, :1]
        live = [
            part(got_ref, 0, 0)[:, :1] < jnp.inf,
            part(got_ref, 0, 1)[:, :1] < jnp.inf,
            mark > -jnp.inf,
            jnp.abs(mark) < jnp.inf,
        ]
        for k in range(4):
            live_ref[k * slots : (k + 1) * slots] = live[k].astype(F32)
    alive = [live_ref[k * slots : (k + 1) * slots] for k in range(4)]
    count = alive[0] + alive[1] + alive[2] + alive[3]
    same = (iota((slots, slots), 0) % cl_dev) == (iota((slots, slots), 1) % cl_dev)
    scale = 1.0 / jnp.sum(jnp.where(same, to_row(count), 0.0), axis=1, keepdims=True)
    half = 2 * slots
    for t, buffer in enumerate(buffers):
        if not first:
            copies[t].wait()
        rows = []
        for core in range(2):
            d0, d1, d3 = [part(buffer, core, k) for k in range(3)]
            if first:
                d0 = jnp.where(live[0], d0, 0.0)
                d1 = jnp.where(live[1], d1, 0.0)
                d3 = jnp.where(live[3], d3, 0.0)
            mean = part(buffer, core, 3) + part(buffer, core, 4)
            if cl_dev % 8 == 0:
                chips = slots // cl_dev
                centroid = jnp.sum((mean * count).reshape(chips, cl_dev, tile), axis=0) * scale[:cl_dev]
                away = (mean.reshape(chips, cl_dev, tile) - centroid[None]).reshape(slots, tile)
            else:
                sums = lax.dot_general(
                    same.astype(F32),
                    mean * count,
                    (((1,), (0,)), ((), ())),
                    precision=lax.Precision.HIGHEST,
                    preferred_element_type=F32,
                )
                centroid = sums * scale
                away = mean - centroid
            centroid_refs[core][:, t * tile : (t + 1) * tile] = centroid[:cl_dev]
            rest = away - (d0 + d1 + d3)
            rows.append(jnp.concatenate([away + d0, away + d1, rest, away + d3], axis=0).astype(BF16))
        every = jnp.concatenate(rows, axis=1)
        upper = lax.dot_general(every[:half], every, (((1,), (1,)), ((), ())), preferred_element_type=F32)
        lower = lax.dot_general(every[half:], every[half:], (((1,), (1,)), ((), ())), preferred_element_type=F32)
        if first:
            gram_ref[:half] = upper
            gram_ref[half:, half:] = lower
            gram_ref[half:, :half] = jnp.zeros((half, half), F32)
        else:
            old_ref = gram_ref if t else gram_in_ref
            gram_ref[:half] = old_ref[:half] + upper
            gram_ref[half:, half:] = old_ref[half:, half:] + lower

    if not first:
        gram_ref[half:, :half] = jnp.transpose(gram_ref[:half, half:])
        n = 4 * slots
        gram = gram_ref[...]
        row = iota((n, n), 0)
        col = iota((n, n), 1)
        diag = jnp.where(row == col, gram, 0.0)
        inv_row = lax.rsqrt(jnp.sum(diag, axis=0, keepdims=True) / width_all + 1e-6)
        inv_col = lax.rsqrt(jnp.sum(diag, axis=1, keepdims=True) / width_all + 1e-6)
        score = gram * inv_col * inv_row / width_all
        usable = ((row % cl_dev) == (col % cl_dev)) & (row != col) & (live_ref[...] > 0.5)
        best = jnp.max(jnp.where(usable, score, -1.0), axis=0, keepdims=True)
        sources = 2 * slots // cl_dev
        place = iota((sources, n), 1)
        source = (place % slots) // cl_dev * 2 + place // (2 * slots)
        spread = jnp.where(source == iota((sources, n), 0), best, 0.0)
        place = iota((n, LANES), 0)
        lane = (place // slots) % 2 * cl_dev + place % cl_dev
        pick = (lane == iota((n, LANES), 1)).astype(F32)
        best_ref[...] = lax.dot_general(
            spread,
            pick,
            (((1,), (0,)), ((), ())),
            precision=lax.Precision.HIGHEST,
            preferred_element_type=F32,
        )


def compare(got, state, cl_dev, width_all, tile):
    first = state is None
    slots = CLUSTERS // 2
    half = got.shape[1] // 5
    chips = slots // cl_dev
    got = got.reshape(chips, 2, cl_dev, got.shape[1])
    if cl_dev % 8:
        got = jnp.moveaxis(got, 1, 0).reshape(1, 2, slots, got.shape[3])
    near = lambda x: pltpu.with_memory_space_constraint(x, pltpu.VMEM)
    vmem = pl.BlockSpec(memory_space=pltpu.VMEM)
    square = jax.ShapeDtypeStruct((4 * slots, 4 * slots), F32)
    out_shape = [jax.ShapeDtypeStruct((cl_dev, half), F32)] * 2
    if first:
        args = [near(got)]
        specs = [vmem]
        out_shape += [square, jax.ShapeDtypeStruct((4 * slots, 1), F32)]
        scratch = []
    else:
        args = [got] + [near(x) for x in state]
        specs = [pl.BlockSpec(memory_space=pl.ANY), vmem, vmem]
        out_shape.append(jax.ShapeDtypeStruct((2 * chips, LANES), F32))
        steps = half // tile
        scratch = [
            pltpu.VMEM(square.shape, F32),
            pltpu.VMEM((steps, *got.shape[:3], 5 * tile), BF16),
            pltpu.SemaphoreType.DMA((steps,)),
        ]
    return pl.pallas_call(
        functools.partial(compare_kernel, cl_dev, width_all, tile, first),
        in_specs=specs,
        out_specs=[vmem] * len(out_shape),
        out_shape=out_shape,
        scratch_shapes=scratch,
        compiler_params=pltpu.CompilerParams(vmem_limit_bytes=VMEM_LIMIT),
    )(*args)


def on_device(embeddings, assignment):
    dev_count = lax.axis_size("rows")
    cl_dev = CLUSTERS // dev_count
    rows, width = embeddings.shape
    core = lax.axis_index("rows") % 2
    exchange = functools.partial(lax.all_to_all, axis_name="rows", split_axis=0, concat_axis=0, tiled=True)
    swap = functools.partial(lax.ppermute, axis_name="rows", perm=[(i, i ^ 1) for i in range(dev_count)])
    mate = swap(assignment)
    first, part, _ = PARTS[0]
    half = part // 2
    head = swap(lax.dynamic_slice_in_dim(embeddings, first + (1 - core) * half, half, 1))
    near = lax.dynamic_slice_in_dim(embeddings, first + core * half, half, 1)
    whole, head, mate, near = lax.optimization_barrier((embeddings, head, mate, near))
    tail = swap(whole)
    got = []
    for start, part, tile in PARTS:
        pair = (embeddings, tail) if got else (near, head)
        coded = code(core.astype(jnp.int32).reshape(1), assignment, mate, *pair, start, part, tile, not got)
        coded, embeddings = lax.optimization_barrier((coded, embeddings))
        got.append(exchange(coded))
    c0, c1, *state = compare(got[0], None, cl_dev, width, PARTS[0][2])
    c2, c3, best = compare(got[1], state, cl_dev, width, PARTS[1][2])
    found = exchange(best)
    row_ids = jnp.arange(rows, dtype=jnp.int32)
    twin = (assignment[:, None] == assignment[None, :]) & (row_ids[None, :] < row_ids[:, None])
    second = jnp.sum(twin.astype(jnp.int32), axis=1)
    owner = (assignment // cl_dev)[:, None] == jnp.arange(dev_count, dtype=jnp.int32)[None, :]
    lane = (second * cl_dev + assignment % cl_dev)[:, None] == jnp.arange(LANES, dtype=jnp.int32)[None, :]
    lines = lax.dot_general(
        owner.astype(F32), found, (((1,), (0,)), ((), ())), precision=lax.Precision.HIGHEST
    )
    maxima = jnp.sum(jnp.where(lane, lines, 0.0), axis=1)
    return (maxima, jnp.concatenate([c2, c3, c0, c1], axis=1))


def solution(mesh):
    placed = (P(("group", "rows"), None), P(("group", "rows")))
    return jax.shard_map(
        on_device,
        mesh=mesh,
        in_specs=placed,
        out_specs=(P(("group", "rows")), P(("group", "rows"), None)),
        check_vma=False,
    )
```

```python
import functools

import jax
import jax.numpy as jnp
from jax import lax
from jax.experimental import pallas as pl
from jax.experimental.pallas import tpu as pltpu
from jax.sharding import PartitionSpec as P

CLUSTERS = 256
LANES = 128
VMEM_LIMIT = 40 * 2**20
PARTS = ((3584, 512, 256), (0, 3584, 896))
F32 = jnp.float32
BF16 = jnp.bfloat16


def iota(shape, axis):
    return lax.broadcasted_iota(jnp.int32, shape, axis)


def mm(a, b):
    return lax.dot_general(a, b, (((1,), (0,)), ((), ())), preferred_element_type=F32)


def to_row(col):
    n = col.shape[0]
    return jnp.sum(jnp.where(iota((n, n), 0) == iota((n, n), 1), col, 0), axis=0, keepdims=True)


def to_col(row):
    n = row.shape[1]
    return jnp.sum(jnp.where(iota((n, n), 0) == iota((n, n), 1), row, 0), axis=1, keepdims=True)


def split(x):
    high = x.astype(BF16)
    return jnp.concatenate([high, (x - high.astype(F32)).astype(BF16)], axis=0)


def code_kernel(mark, core_ref, mine_ref, mate_ref, x_ref, y_ref, out_ref, pick0_ref, pick1_ref, num_ref):
    rows, tile = x_ref.shape
    core = core_ref[0]

    @pl.when(pl.program_id(0) == 0)
    def _():
        mine = mine_ref[...].reshape(1, rows)
        mate = mate_ref[...].reshape(1, rows)
        before = (iota((rows, 1), 0) < iota((1, rows), 1)).astype(F32).astype(BF16)
        counts = []
        for k, pick_ref in enumerate((pick0_ref, pick1_ref)):
            member = iota((CLUSTERS, 1), 0) == jnp.where(core == k, mine, mate)
            marks = member.astype(F32)
            rank = mm(marks.astype(BF16), before)
            second = jnp.where(member, rank, 0.0)
            upper = (marks - second if k == 0 else marks).astype(BF16)
            second = second.astype(BF16)
            for j in range(2):
                cols = slice(j * rows, (j + 1) * rows)
                pick_ref[:CLUSTERS, cols] = upper
                pick_ref[CLUSTERS:, cols] = second
            counts.append(jnp.sum(marks, axis=1, keepdims=True))
        num_ref[:CLUSTERS] = counts[0]
        num_ref[CLUSTERS : 2 * CLUSTERS] = counts[1]
        num_ref[2 * CLUSTERS :] = 1.0 / jnp.maximum(counts[0] + counts[1], 1.0)

    def body(x0_ref, x1_ref):
        rows0 = mm(pick0_ref[...], split(x0_ref[...]))
        rows1 = mm(pick1_ref[...], split(x1_ref[...]))
        count0 = num_ref[:CLUSTERS]
        count1 = num_ref[CLUSTERS : 2 * CLUSTERS]
        row0 = rows0[:CLUSTERS]
        row1 = rows0[CLUSTERS:]
        row3 = rows1[CLUSTERS:]
        mean = ((row0 + row1) + rows1[:CLUSTERS]) * num_ref[2 * CLUSTERS :]
        high = mean.astype(BF16)
        none = jnp.inf if mark else 0.0
        flag = jnp.where(count1 > 0.5, none, -none)
        out_ref[:, :tile] = jnp.where(count0 > 0.5, row0 - mean, none).astype(BF16)
        out_ref[:, tile : 2 * tile] = jnp.where(count0 > 1.5, row1 - mean, none).astype(BF16)
        out_ref[:, 2 * tile : 3 * tile] = jnp.where(count1 > 1.5, row3 - mean, flag).astype(BF16)
        out_ref[:, 3 * tile : 4 * tile] = high
        out_ref[:, 4 * tile :] = (mean - high.astype(F32)).astype(BF16)

    @pl.when(core == 0)
    def _():
        body(x_ref, y_ref)

    @pl.when(core == 1)
    def _():
        body(y_ref, x_ref)


def code(core, mine, mate, x, y, start, width, tile, mark):
    rows = x.shape[0]
    first = start // tile
    steps = width // 2 // tile
    line = pl.BlockSpec((rows,), lambda t, core: (0,))
    block = pl.BlockSpec((rows, tile), lambda t, core: (0, first + core[0] * steps + t))
    if y.shape[1] == tile:
        x, y = [pltpu.with_memory_space_constraint(z, pltpu.VMEM) for z in (x, y)]
        block = pl.BlockSpec(memory_space=pltpu.VMEM)
    return pl.pallas_call(
        functools.partial(code_kernel, mark),
        grid_spec=pltpu.PrefetchScalarGridSpec(
            num_scalar_prefetch=1,
            grid=(steps,),
            in_specs=[line, pl.BlockSpec(memory_space=pltpu.VMEM), block, block],
            out_specs=pl.BlockSpec((CLUSTERS, 5 * tile), lambda t, core: (0, t)),
            scratch_shapes=[
                pltpu.VMEM((2 * CLUSTERS, 2 * rows), BF16),
                pltpu.VMEM((2 * CLUSTERS, 2 * rows), BF16),
                pltpu.VMEM((3 * CLUSTERS, 1), F32),
            ],
        ),
        out_shape=jax.ShapeDtypeStruct((CLUSTERS, steps * 5 * tile), BF16),
    )(core, mine, pltpu.with_memory_space_constraint(mate, pltpu.VMEM), x, y)


def compare_kernel(cl_dev, width_all, tile, first, *refs):
    if first:
        got_ref, *centroid_refs, gram_ref, live_ref = refs
        slots = CLUSTERS // 2
        buffers = [got_ref]
    else:
        got_ref, gram_in_ref, live_ref, *centroid_refs, best_ref, gram_ref, buf_ref, sems = refs
        slots = live_ref.shape[0] // 4
        buffers = [buf_ref.at[t] for t in range(buf_ref.shape[0])]
        copies = [
            pltpu.make_async_copy(got_ref.at[:, :, :, t * 5 * tile : (t + 1) * 5 * tile], buffer, sems.at[t])
            for t, buffer in enumerate(buffers)
        ]
        for copy in copies:
            copy.start()

    def part(buffer, core, k):
        return buffer[:, core, :, k * tile : (k + 1) * tile].astype(F32).reshape(slots, tile)

    if first:
        mark = part(got_ref, 0, 2)[:, :1]
        live = [
            part(got_ref, 0, 0)[:, :1] < jnp.inf,
            part(got_ref, 0, 1)[:, :1] < jnp.inf,
            mark > -jnp.inf,
            jnp.abs(mark) < jnp.inf,
        ]
        for k in range(4):
            live_ref[k * slots : (k + 1) * slots] = live[k].astype(F32)
    alive = [live_ref[k * slots : (k + 1) * slots] for k in range(4)]
    count = alive[0] + alive[1] + alive[2] + alive[3]
    same = (iota((slots, slots), 0) % cl_dev) == (iota((slots, slots), 1) % cl_dev)
    scale = 1.0 / jnp.sum(jnp.where(same, to_row(count), 0.0), axis=1, keepdims=True)
    half = 2 * slots
    for t, buffer in enumerate(buffers):
        if not first:
            copies[t].wait()
        rows = []
        for core in range(2):
            d0, d1, d3 = [part(buffer, core, k) for k in range(3)]
            if first:
                d0 = jnp.where(live[0], d0, 0.0)
                d1 = jnp.where(live[1], d1, 0.0)
                d3 = jnp.where(live[3], d3, 0.0)
            mean = part(buffer, core, 3) + part(buffer, core, 4)
            if cl_dev % 8 == 0:
                chips = slots // cl_dev
                centroid = jnp.sum((mean * count).reshape(chips, cl_dev, tile), axis=0) * scale[:cl_dev]
                away = (mean.reshape(chips, cl_dev, tile) - centroid[None]).reshape(slots, tile)
            else:
                sums = lax.dot_general(
                    same.astype(F32),
                    mean * count,
                    (((1,), (0,)), ((), ())),
                    precision=lax.Precision.HIGHEST,
                    preferred_element_type=F32,
                )
                centroid = sums * scale
                away = mean - centroid
            centroid_refs[core][:, t * tile : (t + 1) * tile] = centroid[:cl_dev]
            rest = away - (d0 + d1 + d3)
            rows.append(jnp.concatenate([away + d0, away + d1, rest, away + d3], axis=0).astype(BF16))
        every = jnp.concatenate(rows, axis=1)
        upper = lax.dot_general(every[:half], every, (((1,), (1,)), ((), ())), preferred_element_type=F32)
        lower = lax.dot_general(every[half:], every[half:], (((1,), (1,)), ((), ())), preferred_element_type=F32)
        if first:
            gram_ref[:half] = upper
            gram_ref[half:, half:] = lower
            gram_ref[half:, :half] = jnp.zeros((half, half), F32)
        else:
            old_ref = gram_ref if t else gram_in_ref
            gram_ref[:half] = old_ref[:half] + upper
            gram_ref[half:, half:] = old_ref[half:, half:] + lower

    if not first:
        gram_ref[half:, :half] = jnp.transpose(gram_ref[:half, half:])
        n = 4 * slots
        gram = gram_ref[...]
        row = iota((n, n), 0)
        col = iota((n, n), 1)
        diag = jnp.where(row == col, gram, 0.0)
        inv_row = lax.rsqrt(jnp.sum(diag, axis=0, keepdims=True) / width_all + 1e-6)
        inv_col = lax.rsqrt(jnp.sum(diag, axis=1, keepdims=True) / width_all + 1e-6)
        score = gram * inv_col * inv_row / width_all
        usable = ((row % cl_dev) == (col % cl_dev)) & (row != col) & (live_ref[...] > 0.5)
        best = jnp.max(jnp.where(usable, score, -1.0), axis=0, keepdims=True)
        device = iota((2 * slots // cl_dev, 1), 0)
        here = device // 2 == iota((1, slots), 1) // cl_dev
        lines = [best[:, k * slots : (k + 1) * slots] for k in range(4)]
        lines = [jnp.where(here, jnp.where(device % 2 == 0, lines[k], lines[k + 2]), 0.0) for k in range(2)]
        best_ref[...] = lines[0] + pltpu.roll(lines[1], slots // 2, 1)


def compare(got, state, cl_dev, width_all, tile):
    first = state is None
    slots = CLUSTERS // 2
    half = got.shape[1] // 5
    chips = slots // cl_dev
    got = got.reshape(chips, 2, cl_dev, got.shape[1])
    if cl_dev % 8:
        got = jnp.moveaxis(got, 1, 0).reshape(1, 2, slots, got.shape[3])
    near = lambda x: pltpu.with_memory_space_constraint(x, pltpu.VMEM)
    vmem = pl.BlockSpec(memory_space=pltpu.VMEM)
    square = jax.ShapeDtypeStruct((4 * slots, 4 * slots), F32)
    out_shape = [jax.ShapeDtypeStruct((cl_dev, half), F32)] * 2
    if first:
        args = [near(got)]
        specs = [vmem]
        out_shape += [square, jax.ShapeDtypeStruct((4 * slots, 1), F32)]
        scratch = []
    else:
        args = [got] + [near(x) for x in state]
        specs = [pl.BlockSpec(memory_space=pl.ANY), vmem, vmem]
        out_shape.append(jax.ShapeDtypeStruct((2 * chips, LANES), F32))
        steps = half // tile
        scratch = [
            pltpu.VMEM(square.shape, F32),
            pltpu.VMEM((steps, *got.shape[:3], 5 * tile), BF16),
            pltpu.SemaphoreType.DMA((steps,)),
        ]
    return pl.pallas_call(
        functools.partial(compare_kernel, cl_dev, width_all, tile, first),
        in_specs=specs,
        out_specs=[vmem] * len(out_shape),
        out_shape=out_shape,
        scratch_shapes=scratch,
        compiler_params=pltpu.CompilerParams(vmem_limit_bytes=VMEM_LIMIT),
    )(*args)


def on_device(embeddings, assignment):
    dev_count = lax.axis_size("rows")
    cl_dev = CLUSTERS // dev_count
    rows, width = embeddings.shape
    core = lax.axis_index("rows") % 2
    exchange = functools.partial(lax.all_to_all, axis_name="rows", split_axis=0, concat_axis=0, tiled=True)
    swap = functools.partial(lax.ppermute, axis_name="rows", perm=[(i, i ^ 1) for i in range(dev_count)])
    mate = swap(assignment)
    first, part, _ = PARTS[0]
    half = part // 2
    head = swap(lax.dynamic_slice_in_dim(embeddings, first + (1 - core) * half, half, 1))
    near = lax.dynamic_slice_in_dim(embeddings, first + core * half, half, 1)
    whole, head, mate, near = lax.optimization_barrier((embeddings, head, mate, near))
    tail = swap(whole)
    got = []
    for start, part, tile in PARTS:
        pair = (embeddings, tail) if got else (near, head)
        coded = code(core.astype(jnp.int32).reshape(1), assignment, mate, *pair, start, part, tile, not got)
        coded, embeddings = lax.optimization_barrier((coded, embeddings))
        got.append(exchange(coded))
    c0, c1, *state = compare(got[0], None, cl_dev, width, PARTS[0][2])
    c2, c3, best = compare(got[1], state, cl_dev, width, PARTS[1][2])
    found = exchange(best)
    row_ids = jnp.arange(rows, dtype=jnp.int32)
    twin = (assignment[:, None] == assignment[None, :]) & (row_ids[None, :] < row_ids[:, None])
    second = jnp.sum(twin.astype(jnp.int32), axis=1)
    owner = (assignment // cl_dev)[:, None] == jnp.arange(dev_count, dtype=jnp.int32)[None, :]
    place = lax.axis_index("rows").astype(jnp.int32) // 2 * cl_dev + assignment % cl_dev + second * (LANES // 2)
    lane = (place % LANES)[:, None] == jnp.arange(LANES, dtype=jnp.int32)[None, :]
    lines = lax.dot_general(
        owner.astype(F32), found, (((1,), (0,)), ((), ())), precision=lax.Precision.HIGHEST
    )
    maxima = jnp.sum(jnp.where(lane, lines, 0.0), axis=1)
    return (maxima, jnp.concatenate([c2, c3, c0, c1], axis=1))


def solution(mesh):
    placed = (P(("group", "rows"), None), P(("group", "rows")))
    return jax.shard_map(
        on_device,
        mesh=mesh,
        in_specs=placed,
        out_specs=(P(("group", "rows")), P(("group", "rows"), None)),
        check_vma=False,
    )
```
